32 devices in a mesh: dp: 8 (over y, x, core), head: 4 (over z).
Axes of the slice: x: 2, y: 2, z: 4, core: 2. Of those that a mesh axis runs over, the one named last changes fastest.
Arguments:
- block_input: bfloat16 [8192, 1536], P(('dp', 'head')), may hold values from -6 to 6
- seq_lengths: int32 [32], P('dp'), may hold values from 1 to 256, 5120 in all
- cotangent: bfloat16 [8192, 1536], P(('dp', 'head')), may hold values from -6 to 6
- norm_gain: float32 [1536], replicated, may hold values from 0.5 to 1.5
- proj_zx: float32 [1536, 2, 3072], P('dp', None, 'head'), may hold values from -0.15625 to 0.15625
- proj_dt: float32 [1536, 48], P('dp', 'head'), may hold values from -0.15625 to 0.15625
- proj_bc: float32 [1536, 256], P('dp'), may hold values from -0.15625 to 0.15625
- chan_params: float32 [6, 3072], P(None, 'head'), may hold values from -2 to 2, as said below
- conv_bc: float32 [5, 256], replicated, may hold values from -3 to 3, as said below
- head_params: float32 [3, 48], P(None, 'head'), may hold values from -5 to 3.2, as said below
- out_proj: float32 [3072, 1536], P(('head', 'dp')), may hold values from -0.109375 to 0.109375
- gain_moments: float32 [2, 1536], replicated, may hold values from -40 to 40, as said below
- zx_moments: float32 [2, 1536, 2, 3072], P(None, 'dp', None, 'head'), may hold values from -40 to 40, as said below
- dt_moments: float32 [2, 1536, 48], P(None, 'dp', 'head'), may hold values from -40 to 40, as said below
- bc_moments: float32 [2, 1536, 256], P(None, 'dp'), may hold values from -40 to 40, as said below
- chan_moments: float32 [2, 6, 3072], P(None, None, 'head'), may hold values from -40 to 40, as said below
- convbc_moments: float32 [2, 5, 256], replicated, may hold values from -40 to 40, as said below
- head_moments: float32 [2, 3, 48], P(None, None, 'head'), may hold values from -40 to 40, as said below
- out_moments: float32 [2, 3072, 1536], P(None, ('head', 'dp')), may hold values from -40 to 40, as said below
Outputs:
- block_output: bfloat16 [8192, 1536], P(('dp', 'head'))
- input_grad: float32 [8192, 1536], P(('dp', 'head'))
- gain_next: float32 [1536], replicated
- gain_state: float32 [2, 1536], replicated
- zx_next: float32 [1536, 2, 3072], P('dp', None, 'head')
- zx_state: float32 [2, 1536, 2, 3072], P(None, 'dp', None, 'head')
- dt_next: float32 [1536, 48], P('dp', 'head')
- dt_state: float32 [2, 1536, 48], P(None, 'dp', 'head')
- bc_next: float32 [1536, 256], P('dp')
- bc_state: float32 [2, 1536, 256], P(None, 'dp')
- chan_next: float32 [6, 3072], P(None, 'head')
- chan_state: float32 [2, 6, 3072], P(None, None, 'head')
- convbc_next: float32 [5, 256], replicated
- convbc_state: float32 [2, 5, 256], replicated
- head_next: float32 [3, 48], P(None, 'head')
- head_state: float32 [2, 3, 48], P(None, None, 'head')
- outproj_next: float32 [3072, 1536], P(('head', 'dp'))
- outproj_state: float32 [2, 3072, 1536], P(None, ('head', 'dp'))
The draws below stay inside these ranges and needn't reach their ends.
Inputs may be any that keep to these rules, and one draw needn't show every extreme that they name: Each padded sequence is live on its first seq_lengths positions; the lengths sum to 5120 and some sequence is live on all 256 positions. `chan_params`: taps in -2 to 2, bias in -0.5 to 0.5, gate gains in 0.5 to 1.5. `conv_bc`: taps and biases of B and C. `head_params`: A_log in -3 to 3.2, step bias in -5 to -1, skip coefficient in 0.5 to 1.5. `gain_moments`: root second moments lie in 3 to 40. `zx_moments`: root second moments lie in 3 to 40. `dt_moments`: root second moments lie in 3 to 40. `bc_moments`: root second moments lie in 3 to 40. `chan_moments`: root second moments lie in 3 to 40. `convbc_moments`: root second moments lie in 3 to 40. `head_moments`: root second moments lie in 3 to 40. `out_moments`: root second moments lie in 3 to 40.
All inputs are finite; a program needn't handle non-finite values. No bound on the sum of `seq_lengths` on one device may be relied on, other than what follows from the above.
Results may differ from the reference program's by a relative error of at most 0.012.
Values may be sent and summed in bfloat16 or wider, within the bound.
No kernel may reach another device: no remote copies, remote signals or barrier semaphores. Data moves between devices by JAX's collectives and lax.ppermute only.
A program may use at most 128 MiB of HBM per device.

```python
import math
import jax
import jax.numpy as jnp
import numpy as np
from jax import lax

D = 1536
HEADS = 48
STATE = 128
KERNEL = 4
SEQLEN = 256
SLOTS = 4
INNER = 3072
SEQS = 32
TOKENS = 8192
N_DP = 8


def moment_pair(key, shape):
    first_key, second_key = jax.random.split(key)
    first_mom = 10.0 * jax.random.truncated_normal(first_key, -4.0, 4.0, shape, jnp.float32)
    log_root = jax.random.uniform(second_key, shape, jnp.float32, jnp.log(3.0), jnp.log(40.0))
    second_root = jnp.clip(jnp.exp(log_root), 3.0, 40.0)
    return jnp.stack([first_mom, second_root])


def draw_chan_params(key, part):
    tap_key, bias_key, gain_key = jax.random.split(key, 3)
    tap_rows = 0.5 * jax.random.truncated_normal(tap_key, -4.0, 4.0, (KERNEL, INNER), jnp.float32)
    bias_row = jax.random.uniform(bias_key, (1, INNER), jnp.float32, -0.5, 0.5)
    gain_row = jax.random.uniform(gain_key, (1, INNER), jnp.float32, 0.5, 1.5)
    return jnp.concatenate([tap_rows, bias_row, gain_row], axis=0)


def draw_conv_bc(key, part):
    tap_key, bias_key = jax.random.split(key)
    tap_rows = 0.5 * jax.random.truncated_normal(tap_key, -4.0, 4.0, (KERNEL, 2 * STATE), jnp.float32)
    bias_row = 0.5 * jax.random.truncated_normal(bias_key, -6.0, 6.0, (1, 2 * STATE), jnp.float32)
    return jnp.concatenate([tap_rows, bias_row], axis=0)


def draw_head_params(key, part):
    log_key, bias_key, skip_key = jax.random.split(key, 3)
    skip_row = jax.random.uniform(skip_key, (1, HEADS), jnp.float32, 0.5, 1.5)
    log_row = jax.random.uniform(log_key, (1, HEADS), jnp.float32, -1.0, 2.2)
    bias_row = jax.random.uniform(bias_key, (1, HEADS), jnp.float32, -5.0, -1.0)
    return jnp.concatenate([log_row, bias_row, skip_row], axis=0)


def draw_gain_moments(key, part):
    return moment_pair(key, (D,))


def draw_zx_moments(key, part):
    return moment_pair(key, (D, 2, INNER))


def draw_dt_moments(key, part):
    return moment_pair(key, (D, HEADS))


def draw_bc_moments(key, part):
    return moment_pair(key, (D, 2 * STATE))


def draw_chan_moments(key, part):
    return moment_pair(key, (KERNEL + 2, INNER))


def draw_convbc_moments(key, part):
    return moment_pair(key, (KERNEL + 1, 2 * STATE))


def draw_head_moments(key, part):
    return moment_pair(key, (3, HEADS))


def draw_out_moments(key, part):
    return moment_pair(key, (INNER, D))


def level_of(key, extent, cuts, low, high):
    def one(position, parts):
        draws = jax.random.uniform(jax.random.fold_in(jax.random.fold_in(key, 6), position), (parts,), jnp.float32, low / len(cuts), high / len(cuts))
        return jnp.repeat(jnp.exp(draws), extent[position] // parts).reshape((-1,) + (1,) * (len(extent) - position - 1))

    loudness = one(*cuts[0])
    for cut in cuts[1:]:
        loudness = loudness * one(*cut)
    return loudness


def length_profile(count, total, most, skew):
    portions = [(1 << 20) // math.isqrt(rank ** skew) + 1 for rank in range(2, count + 1)]
    surplus, counts = total - most - (count - 1), [1] * (count - 1)
    while surplus > 0:
        free = [i for i in range(count - 1) if counts[i] < most]
        whole, budget = sum([portions[i] for i in free]), surplus
        for i in free:
            addition = min(most - counts[i], max(1, budget * portions[i] // whole), surplus)
            counts[i] = counts[i] + addition
            surplus = surplus - addition
    return np.array([most] + counts)


def ragged(stream_key, amount, total, bound, skew):
    if amount == 2:
        one = jax.random.randint(stream_key, (), max(1, total - bound), min(bound, total - 1) + 1)
        return jnp.stack([one, total - one])
    tallies = jnp.asarray(length_profile(amount, total, bound, skew), jnp.int32)
    twos = (amount - 1) // 2
    giver, sink = tallies[1:1 + 2 * twos:2], tallies[2:2 + 2 * twos:2]
    slack = jnp.minimum(giver - 1, bound - sink)
    shifted = jax.random.randint(jax.random.fold_in(stream_key, 1), (twos,), 0, 1 << 20) % (slack + 1)
    tallies = tallies.at[1:1 + 2 * twos:2].set(giver - shifted).at[2:2 + 2 * twos:2].set(sink + shifted)
    return tallies[jax.random.permutation(jax.random.fold_in(stream_key, 2), amount)]


def normal_values(own_key, shape, deviation, bound, cuts=(), held_as=jnp.bfloat16):
    array = deviation * jax.random.normal(own_key, shape, jnp.float32)
    if cuts:
        array = array * level_of(own_key, shape, cuts, -0.22, 0.18)
    return jnp.clip(array, -bound, bound).astype(held_as)


def setup_inputs(seed: int = 0) -> dict:
    streams_of = jax.random.split(jax.random.key(seed), 20)
    block_input = normal_values(streams_of[0], (TOKENS, D), 1.0, 6.0, ((0, 32),))
    seq_lengths = ragged(streams_of[1], SEQS, SEQS * SEQLEN * 5 // 8, SEQLEN, 2).astype(jnp.int32)
    cotangent = normal_values(streams_of[2], (TOKENS, D), 1.0, 6.0, ((0, 32),))
    norm_gain = jnp.clip(1.0 + 0.1 * jax.random.normal(streams_of[3], (D,), jnp.float32), 0.5, 1.5)
    proj_zx = normal_values(streams_of[4], (D, 2, INNER), D ** -0.5, 0.15625, ((0, 8), (2, 4)), jnp.float32)
    proj_dt = normal_values(streams_of[5], (D, HEADS), D ** -0.5, 0.15625, ((0, 8), (1, 4)), jnp.float32)
    proj_bc = normal_values(streams_of[6], (D, 2 * STATE), D ** -0.5, 0.15625, ((0, 8),), jnp.float32)
    chan_params = draw_chan_params(jax.random.fold_in(streams_of[19], 71), 0)
    conv_bc = draw_conv_bc(jax.random.fold_in(streams_of[19], 71), 0)
    head_params = draw_head_params(jax.random.fold_in(streams_of[19], 71), 0)
    out_proj = normal_values(streams_of[10], (INNER, D), INNER ** -0.5, 0.109375, ((0, 32),), jnp.float32)
    gain_moments = draw_gain_moments(jax.random.fold_in(streams_of[19], 71), 0)
    zx_moments = draw_zx_moments(jax.random.fold_in(streams_of[19], 71), 0)
    dt_moments = draw_dt_moments(jax.random.fold_in(streams_of[19], 71), 0)
    bc_moments = draw_bc_moments(jax.random.fold_in(streams_of[19], 71), 0)
    chan_moments = draw_chan_moments(jax.random.fold_in(streams_of[19], 71), 0)
    convbc_moments = draw_convbc_moments(jax.random.fold_in(streams_of[19], 71), 0)
    head_moments = draw_head_moments(jax.random.fold_in(streams_of[19], 71), 0)
    out_moments = draw_out_moments(jax.random.fold_in(streams_of[19], 71), 0)
    return dict(block_input=block_input, seq_lengths=seq_lengths, cotangent=cotangent, norm_gain=norm_gain, proj_zx=proj_zx, proj_dt=proj_dt, proj_bc=proj_bc, chan_params=chan_params, conv_bc=conv_bc, head_params=head_params, out_proj=out_proj, gain_moments=gain_moments, zx_moments=zx_moments, dt_moments=dt_moments, bc_moments=bc_moments, chan_moments=chan_moments, convbc_moments=convbc_moments, head_moments=head_moments, out_moments=out_moments)


norm_eps = 1e-05
beta_one = 0.9
beta_two = 0.95
adam_eps = 1e-08
step_count = 3.0
rate_matrix = 0.005
rate_vector = 0.2
weight_decay = 0.1
highest = lax.Precision.HIGHEST

def causal(values, tap_rows):
    kernel = tap_rows.shape[0] - 1
    length = values.shape[0]
    padded = jnp.pad(values, ((kernel - 1, 0), (0, 0)))
    summed = jnp.broadcast_to(tap_rows[kernel][None, :], values.shape)
    for offset in range(kernel):
        summed = summed + tap_rows[offset][None, :] * padded[offset:offset + length]
    return summed

def mixer_slot(proj_rows, bc_rows, step_raw, conv_taps, conv_shared, head_table):
    length = proj_rows.shape[0]
    inner_loc = conv_taps.shape[1]
    heads_loc = head_table.shape[1]
    headdim = inner_loc // heads_loc
    state_dim = bc_rows.shape[1] // 2
    gate_pre = proj_rows[:, :inner_loc]
    conv_x = jax.nn.silu(causal(proj_rows[:, inner_loc:], conv_taps))
    shared = jax.nn.silu(causal(bc_rows, conv_shared))
    input_map = shared[:, :state_dim]
    output_map = shared[:, state_dim:]
    step_size = jax.nn.softplus(step_raw + head_table[1][None, :])
    decay_rate = -jnp.exp(head_table[0])
    row_pos = lax.broadcasted_iota(jnp.int32, (length, length), 0)
    col_pos = lax.broadcasted_iota(jnp.int32, (length, length), 1)
    causal_mask = row_pos >= col_pos
    lower_ones = causal_mask.astype(jnp.float32)
    cum_log = jnp.dot(lower_ones, step_size * decay_rate[None, :], precision=highest).T
    log_gap = cum_log[:, :, None] - cum_log[:, None, :]
    decay_mat = jnp.exp(jnp.where(causal_mask[None], log_gap, -1e+30))
    scores = jnp.dot(output_map, input_map.T, precision=highest)
    weights = scores[None] * decay_mat * step_size.T[:, None, :]
    head_values = conv_x.reshape(length, heads_loc, headdim)
    output = jnp.einsum('hts,shp->thp', weights, head_values, precision=highest)
    output = output + head_table[2][None, :, None] * head_values
    return output.reshape(length, inner_loc) * jax.nn.silu(gate_pre)

def adam_update(parameter, moments, gradient, learn_rate, decay_coef):
    first_mom = beta_one * moments[0] + (1.0 - beta_one) * gradient
    second_mom = beta_two * moments[1] * moments[1] + (1.0 - beta_two) * gradient * gradient
    second_root = jnp.sqrt(second_mom)
    first_hat = first_mom / (1.0 - beta_one ** step_count)
    second_hat = second_mom / (1.0 - beta_two ** step_count)
    updated = parameter - learn_rate * (first_hat / (jnp.sqrt(second_hat) + adam_eps) + decay_coef * parameter)
    return (updated, jnp.stack([first_mom, second_root]))

def reference(block_input, seq_lengths, cotangent, norm_gain, proj_zx, proj_dt, proj_bc, chan_params, conv_bc, head_params, out_proj, gain_moments, zx_moments, dt_moments, bc_moments, chan_moments, convbc_moments, head_moments, out_moments):
    rows_blk = SLOTS * SEQLEN
    gain_float = lax.optimization_barrier(norm_gain.astype(jnp.bfloat16)).astype(jnp.float32)
    zx_mat = proj_zx.astype(jnp.bfloat16).reshape(D, 2 * INNER)
    dt_mat = proj_dt.astype(jnp.bfloat16)
    bc_mat = proj_bc.astype(jnp.bfloat16)
    out_mat = out_proj.astype(jnp.bfloat16)
    conv_taps = chan_params[:KERNEL + 1]
    gate_gain = chan_params[KERNEL + 1]
    positions = lax.broadcasted_iota(jnp.int32, (SEQS, SEQLEN), 1)
    live_all = (positions < seq_lengths[:, None]).astype(jnp.float32).reshape(N_DP, rows_blk, 1)
    input_blocks = block_input.reshape(N_DP, rows_blk, D)
    cot_blocks = cotangent.reshape(N_DP, rows_blk, D)

    def one_block(totals, members):
        input_rows, cot_rows, live_mask = members
        input_float = input_rows.astype(jnp.float32)
        inv_norm = lax.rsqrt(lax.optimization_barrier(jnp.mean(input_float * input_float, axis=-1, keepdims=True)) + norm_eps)
        input_hat = input_float * inv_norm
        normed_in = (input_hat * gain_float[None, :]).astype(jnp.bfloat16)
        proj_out = jnp.dot(normed_in, zx_mat, preferred_element_type=jnp.float32)
        step_raw = jnp.dot(normed_in, dt_mat, preferred_element_type=jnp.float32)
        bc_out = jnp.dot(normed_in, bc_mat, preferred_element_type=jnp.float32)
        proj_slots = proj_out.reshape(SLOTS, SEQLEN, 2 * INNER)
        bc_slots = bc_out.reshape(SLOTS, SEQLEN, 2 * STATE)
        step_slots = step_raw.reshape(SLOTS, SEQLEN, HEADS)

        def forward_slot(members_slot):
            return mixer_slot(members_slot[0], members_slot[1], members_slot[2], conv_taps, conv_bc, head_params)
        gated_rows = lax.map(forward_slot, (proj_slots, bc_slots, step_slots)).reshape(rows_blk, INNER)
        inv_gate = lax.rsqrt(lax.optimization_barrier(jnp.sum(gated_rows * gated_rows, axis=-1, keepdims=True)) / INNER + norm_eps)
        normed_out = (gated_rows * inv_gate * gate_gain[None, :]).astype(jnp.bfloat16)
        branch = jnp.dot(normed_out, out_mat, preferred_element_type=jnp.float32)
        block_output = (input_float + live_mask * branch).astype(jnp.bfloat16)
        cot_live = (cot_rows.astype(jnp.float32) * live_mask).astype(jnp.bfloat16)
        grad_normed = jnp.dot(cot_live, out_mat.T, preferred_element_type=jnp.float32)
        grad_out = jnp.dot(normed_out.T, cot_live, preferred_element_type=jnp.float32)
        grad_gate = lax.optimization_barrier(jnp.sum(grad_normed * gated_rows * inv_gate, axis=0))
        scaled = grad_normed * gate_gain[None, :]
        cross_sum = lax.optimization_barrier(jnp.sum(scaled * gated_rows, axis=-1, keepdims=True))
        grad_gated = inv_gate * scaled - gated_rows * inv_gate ** 3 * cross_sum / INNER

        def backward_slot(slot_totals, members_slot):
            unused, pullback = jax.vjp(mixer_slot, members_slot[0], members_slot[1], members_slot[2], conv_taps, conv_bc, head_params)
            pieces = pullback(members_slot[3])
            return ((slot_totals[0] + pieces[3], slot_totals[1] + pieces[4], slot_totals[2] + pieces[5]), (pieces[0], pieces[1], pieces[2]))
        zero_slot = (jnp.zeros_like(conv_taps), jnp.zeros_like(conv_bc), jnp.zeros_like(head_params))
        slot_grads, slot_cots = lax.scan(backward_slot, zero_slot, (proj_slots, bc_slots, step_slots, grad_gated.reshape(SLOTS, SEQLEN, INNER)))
        cot_proj = slot_cots[0].reshape(rows_blk, 2 * INNER).astype(jnp.bfloat16)
        cot_bc = slot_cots[1].reshape(rows_blk, 2 * STATE).astype(jnp.bfloat16)
        cot_step = slot_cots[2].reshape(rows_blk, HEADS).astype(jnp.bfloat16)
        cot_input = jnp.dot(cot_proj, zx_mat.T, preferred_element_type=jnp.float32)
        cot_input = cot_input + jnp.dot(cot_step, dt_mat.T, preferred_element_type=jnp.float32)
        cot_input = cot_input + jnp.dot(cot_bc, bc_mat.T, preferred_element_type=jnp.float32)
        grad_zx = jnp.dot(normed_in.T, cot_proj, preferred_element_type=jnp.float32)
        grad_dt = jnp.dot(normed_in.T, cot_step, preferred_element_type=jnp.float32)
        grad_bc = jnp.dot(normed_in.T, cot_bc, preferred_element_type=jnp.float32)
        row_dot = lax.optimization_barrier(jnp.sum(cot_input * gain_float[None, :] * input_hat, axis=-1, keepdims=True))
        input_grad = cot_rows.astype(jnp.float32) + inv_norm * (cot_input * gain_float[None, :] - input_hat * row_dot / D)
        grad_gain = lax.optimization_barrier(jnp.sum(cot_input * input_hat, axis=0))
        fresh = (grad_gain, grad_zx, grad_dt, grad_bc, slot_grads[0], grad_gate, slot_grads[1], slot_grads[2], grad_out)
        return (tuple((old + new for old, new in zip(totals, fresh))), (block_output, input_grad))
    start = (jnp.zeros((D,), jnp.float32), jnp.zeros((D, 2 * INNER), jnp.float32), jnp.zeros((D, HEADS), jnp.float32), jnp.zeros((D, 2 * STATE), jnp.float32), jnp.zeros((KERNEL + 1, INNER), jnp.float32), jnp.zeros((INNER,), jnp.float32), jnp.zeros((KERNEL + 1, 2 * STATE), jnp.float32), jnp.zeros((3, HEADS), jnp.float32), jnp.zeros((INNER, D), jnp.float32))
    totals, results = lax.scan(one_block, start, (input_blocks, cot_blocks, live_all))
    block_output = results[0].reshape(TOKENS, D)
    input_grad = results[1].reshape(TOKENS, D)
    grad_chan = jnp.concatenate([totals[4], totals[5][None, :]], axis=0)
    gain_next, gain_state = adam_update(norm_gain, gain_moments, totals[0], rate_vector, 0.0)
    zx_next, zx_state = adam_update(proj_zx, zx_moments, totals[1].reshape(D, 2, INNER), rate_matrix, weight_decay)
    dt_next, dt_state = adam_update(proj_dt, dt_moments, totals[2], rate_matrix, weight_decay)
    bc_next, bc_state = adam_update(proj_bc, bc_moments, totals[3], rate_matrix, weight_decay)
    chan_next, chan_state = adam_update(chan_params, chan_moments, grad_chan, rate_vector, 0.0)
    convbc_next, convbc_state = adam_update(conv_bc, convbc_moments, totals[6], rate_vector, 0.0)
    head_next, head_state = adam_update(head_params, head_moments, totals[7], rate_vector, 0.0)
    outproj_next, outproj_state = adam_update(out_proj, out_moments, totals[8], rate_matrix, weight_decay)
    return (block_output, input_grad, gain_next, gain_state, zx_next, zx_state, dt_next, dt_state, bc_next, bc_state, chan_next, chan_state, convbc_next, convbc_state, head_next, head_state, outproj_next, outproj_state)
```

```python
import functools

import jax
import jax.numpy as jnp
from jax import lax
from jax.experimental import pallas as pl
from jax.experimental.pallas import tpu as pltpu
from jax.sharding import PartitionSpec as P

norm_eps = 1e-05
beta_one = 0.9
beta_two = 0.95
adam_eps = 1e-08
step_count = 3.0
rate_matrix = 0.005
rate_vector = 0.2
weight_decay = 0.1
lanes = 128
sub = 8
f32 = jnp.float32
bf16 = jnp.bfloat16


def dot(lhs, rhs, over=(1, 0)):
    return lax.dot_general(
        lhs, rhs, (((over[0],), (over[1],)), ((), ())), preferred_element_type=f32
    )


def dot_exact(lhs, rhs, over=(1, 0)):
    return lax.dot_general(
        lhs,
        rhs,
        (((over[0],), (over[1],)), ((), ())),
        precision=lax.Precision.HIGHEST,
        preferred_element_type=f32,
    )


def iota(shape, axis):
    return lax.broadcasted_iota(jnp.int32, shape, axis)


def later(values, count):
    if count == 0:
        return values
    rolled = pltpu.roll(values, count, 0)
    return jnp.where(iota(values.shape, 0) >= count, rolled, 0.0)


def earlier(values, count):
    if count == 0:
        return values
    length = values.shape[0]
    rolled = pltpu.roll(values, length - count, 0)
    return jnp.where(iota(values.shape, 0) < length - count, rolled, 0.0)


def conv(values, taps, kernel):
    summed = taps[kernel : kernel + 1] + taps[kernel - 1 : kernel] * values
    for offset in range(kernel - 1):
        summed = summed + taps[offset : offset + 1] * later(values, kernel - 1 - offset)
    return summed


def conv_back(grads, taps, kernel):
    summed = taps[kernel - 1 : kernel] * grads
    for offset in range(kernel - 1):
        summed = summed + taps[offset : offset + 1] * earlier(grads, kernel - 1 - offset)
    return summed


def conv_sums(grads, values, kernel):
    rows = [
        jnp.sum(grads * later(values, kernel - 1 - offset), axis=0, keepdims=True)
        for offset in range(kernel)
    ]
    rows.append(jnp.sum(grads, axis=0, keepdims=True))
    return rows


def sigmoid(values):
    return 1.0 / (1.0 + jnp.exp(-values))


def shared_parts(proj_ref, cbc_ref, head_ref, inner, state, kernel):
    bc_rows = proj_ref[:, 2 * inner : 2 * inner + 2 * state]
    step_raw = proj_ref[:, 2 * inner + 2 * state :] + head_ref[1:2, :]
    length = bc_rows.shape[0]
    bc_pre = conv(bc_rows, cbc_ref, kernel)
    bc_sig = sigmoid(bc_pre)
    shared = bc_pre * bc_sig
    step = jnp.maximum(step_raw, 0.0) + jnp.log1p(jnp.exp(-jnp.abs(step_raw)))
    rate = -jnp.exp(head_ref[0:1, :])
    lower = (iota((length, length), 0) >= iota((length, length), 1)).astype(f32)
    cum = dot_exact(lower, step * rate)
    in_map = shared[:, :state].astype(bf16)
    out_map = shared[:, state:].astype(bf16)
    scores = dot(out_map, in_map, (1, 1)) * lower
    return dict(
        bc_rows=bc_rows,
        bc_pre=bc_pre,
        bc_sig=bc_sig,
        step_raw=step_raw,
        step=step,
        rate=rate,
        cum=cum,
        cum_t=cum.T,
        in_map=in_map,
        out_map=out_map,
        scores=scores,
    )


def pick(values, pair, first):
    return jnp.where(
        first, values[:, 2 * pair : 2 * pair + 1], values[:, 2 * pair + 1 : 2 * pair + 2]
    )


def blocks_of(length):
    half = length // 2
    return [((0, half), (0, half)), ((half, length), (0, length))]


def forward_kernel(
    x_ref, w_ref, taps_ref, cbc_ref, head_ref, proj_ref, y_ref, gated_ref, *, inner, state, kernel
):
    length = x_ref.shape[0]
    width = w_ref.shape[1]
    rows = x_ref[...]
    for start in range(0, width, 256):
        stop = min(width, start + 256)
        proj_ref[:, start:stop] = dot(rows, w_ref[:, start:stop])
    part = shared_parts(proj_ref, cbc_ref, head_ref, inner, state, kernel)
    step, cum, cum_t, scores = part["step"], part["cum"], part["cum_t"], part["scores"]
    first = iota((length, lanes), 1) < lanes // 2
    for pair in range(inner // lanes):
        cols = slice(pair * lanes, (pair + 1) * lanes)
        taps = taps_ref[:, cols]
        gate = proj_ref[:, cols]
        values = conv(
            proj_ref[:, inner + pair * lanes : inner + (pair + 1) * lanes], taps, kernel
        )
        values = values * sigmoid(values)
        scaled = values * pick(step, pair, first)
        halves = (
            jnp.where(first, scaled, 0.0).astype(bf16),
            jnp.where(first, 0.0, scaled).astype(bf16),
        )
        pieces = []
        for (r0, r1), (c0, c1) in blocks_of(length):
            total = None
            for side in range(2):
                head = 2 * pair + side
                gap = cum[r0:r1, head : head + 1] - cum_t[head : head + 1, c0:c1]
                weights = (scores[r0:r1, c0:c1] * jnp.exp(jnp.minimum(gap, 0.0))).astype(bf16)
                term = dot(weights, halves[side][c0:c1])
                total = term if total is None else total + term
            pieces.append(total)
        output = jnp.concatenate(pieces, axis=0)
        y_ref[:, cols] = output
        gated_ref[:, cols] = (output + taps[kernel + 2 : kernel + 3] * values) * (
            gate * sigmoid(gate)
        )


def gate_kernel(cot_ref, out_ref, gated_ref, taps_ref, grad_ref, stats_ref, branch_ref, *, kernel):
    gain = taps_ref[kernel + 1 : kernel + 2, :]
    weights = out_ref[...]
    grad = dot(cot_ref[...], weights, (1, 1))
    grad_ref[...] = grad
    gated = gated_ref[...]
    lifted = gated * gain
    branch_ref[...] = dot(lifted.astype(bf16), weights).astype(bf16)
    ones = jnp.ones((sub, gated.shape[1]), f32)
    squares = dot_exact(ones, gated * gated, (1, 1))
    cross = dot_exact(ones, grad * lifted, (1, 1))
    stats_ref[...] = jnp.where(iota(squares.shape, 0) == 0, squares, cross)


def backward_kernel(
    *refs, inner, state, kernel, inner_all, stat_parts
):
    stat_refs = refs[:stat_parts]
    (
        proj_ref,
        y_ref,
        grad_ref,
        taps_ref,
        cbc_ref,
        head_ref,
        cot_ref,
        normed_ref,
        tap_sums_ref,
        cbc_sums_ref,
        head_sums_ref,
        score_ref,
    ) = refs[stat_parts:]
    length = proj_ref.shape[0]
    half_lanes = lanes // 2

    @pl.when(pl.program_id(0) == 0)
    def clear():
        tap_sums_ref[...] = jnp.zeros(tap_sums_ref.shape, f32)
        cbc_sums_ref[...] = jnp.zeros(cbc_sums_ref.shape, f32)
        head_sums_ref[...] = jnp.zeros(head_sums_ref.shape, f32)

    stats = stat_refs[0][...]
    for more in stat_refs[1:]:
        stats = stats + more[...]
    unit = (iota((length, length), 0) == iota((length, length), 1)).astype(f32)
    columns = dot_exact(unit, stats, (1, 1))
    inv = lax.rsqrt(columns[:, 0:1] / inner_all + norm_eps)
    pull = inv * inv * inv * columns[:, 1:2] / inner_all

    part = shared_parts(proj_ref, cbc_ref, head_ref, inner, state, kernel)
    step, cum, cum_t, scores = part["step"], part["cum"], part["cum_t"], part["scores"]
    first = iota((length, lanes), 1) < half_lanes
    score_ref[...] = jnp.zeros(score_ref.shape, f32)
    cum_grad = jnp.zeros((length, lanes), f32)
    step_grad = jnp.zeros((length, lanes), f32)
    for pair in range(inner // lanes):
        cols = slice(pair * lanes, (pair + 1) * lanes)
        xcols = slice(inner + pair * lanes, inner + (pair + 1) * lanes)
        taps = taps_ref[:, cols]
        gain = taps[kernel + 1 : kernel + 2]
        skip = taps[kernel + 2 : kernel + 3]
        gate = proj_ref[:, cols]
        raw = proj_ref[:, xcols]
        pre = conv(raw, taps, kernel)
        pre_sig = sigmoid(pre)
        values = pre * pre_sig
        spread = pick(step, pair, first)
        scaled = values * spread
        gate_sig = sigmoid(gate)
        lift = gate * gate_sig
        plain = y_ref[:, cols]
        output = plain + skip * values
        gated = output * lift
        normed = gated * inv
        grad = grad_ref[:, cols]
        normed_ref[:, cols] = (normed * gain).astype(bf16)
        gain_row = jnp.sum(grad * normed, axis=0, keepdims=True)
        gated_grad = inv * (grad * gain) - gated * pull
        cot_ref[:, cols] = (
            gated_grad * output * (gate_sig * (1.0 + gate * (1.0 - gate_sig)))
        ).astype(bf16)
        out_grad = gated_grad * lift
        skip_row = jnp.sum(out_grad * values, axis=0, keepdims=True)
        out_low = out_grad.astype(bf16)
        scaled_low = scaled.astype(bf16)
        zero = jnp.zeros_like(out_low)
        sides = (jnp.where(first, out_low, zero), jnp.where(first, zero, out_low))
        half = length // 2
        pulled = [jnp.zeros((half, lanes), f32), jnp.zeros((half, lanes), f32)]
        for (r0, r1), (c0, c1) in blocks_of(length):
            score_sum = score_ref[r0:r1, c0:c1]
            for side in range(2):
                head = 2 * pair + side
                gap = cum[r0:r1, head : head + 1] - cum_t[head : head + 1, c0:c1]
                decay = jnp.exp(jnp.minimum(gap, 0.0))
                weights = (scores[r0:r1, c0:c1] * decay).astype(bf16)
                score_sum = score_sum + dot(sides[side][r0:r1], scaled_low[c0:c1], (1, 1)) * decay
                back = dot(weights, sides[side][r0:r1], (0, 0))
                pulled[0] = pulled[0] + back[:half]
                if c1 > half:
                    pulled[1] = pulled[1] + back[half:]
            score_ref[r0:r1, c0:c1] = score_sum
        scaled_grad = jnp.concatenate(pulled, axis=0)
        hot = (
            2 * pair + (iota((lanes, lanes), 0) >= half_lanes).astype(jnp.int32)
            == iota((lanes, lanes), 1)
        ).astype(f32)
        balance = out_low.astype(f32) * plain - scaled_low.astype(f32) * scaled_grad
        cum_grad = cum_grad + dot_exact(balance, hot)
        step_grad = step_grad + dot_exact(values * scaled_grad, hot)
        value_grad = skip * out_grad + scaled_grad * spread
        pre_grad = value_grad * (pre_sig * (1.0 + pre * (1.0 - pre_sig)))
        cot_ref[:, xcols] = conv_back(pre_grad, taps, kernel).astype(bf16)
        rows = conv_sums(pre_grad, raw, kernel) + [gain_row, skip_row]
        rows = rows + [jnp.zeros_like(gain_row)] * (tap_sums_ref.shape[0] - len(rows))
        tap_sums_ref[:, cols] = tap_sums_ref[:, cols] + jnp.concatenate(rows, axis=0)

    lower = iota((length, length), 0) >= iota((length, length), 1)
    score_low = jnp.where(lower, score_ref[...], 0.0).astype(bf16)
    shared_grad = jnp.concatenate(
        [dot(score_low, part["out_map"], (0, 0)), dot(score_low, part["in_map"])], axis=1
    )
    bc_pre, bc_sig = part["bc_pre"], part["bc_sig"]
    bc_grad = shared_grad * (bc_sig * (1.0 + bc_pre * (1.0 - bc_sig)))
    cot_ref[:, 2 * inner : 2 * inner + 2 * state] = conv_back(bc_grad, cbc_ref, kernel).astype(bf16)
    rows = conv_sums(bc_grad, part["bc_rows"], kernel)
    rows = rows + [jnp.zeros_like(rows[0])] * (cbc_sums_ref.shape[0] - len(rows))
    cbc_sums_ref[...] = cbc_sums_ref[...] + jnp.concatenate(rows, axis=0)
    decay_grad = dot_exact(lower.astype(f32), cum_grad, (0, 0))
    raw_grad = (step_grad + decay_grad * part["rate"]) * sigmoid(part["step_raw"])
    cot_ref[:, 2 * inner + 2 * state :] = raw_grad.astype(bf16)
    rows = [
        part["rate"] * jnp.sum(step * decay_grad, axis=0, keepdims=True),
        jnp.sum(raw_grad, axis=0, keepdims=True),
    ]
    rows = rows + [jnp.zeros_like(rows[0])] * (head_sums_ref.shape[0] - len(rows))
    head_sums_ref[...] = head_sums_ref[...] + jnp.concatenate(rows, axis=0)


def whole(array):
    return pl.BlockSpec(array.shape, lambda step: (0,) * array.ndim, pipeline_mode=pl.Buffered(1))


def rows_spec(length, width):
    return pl.BlockSpec((length, width), lambda step: (step, 0))


def stat_spec(length, slots, back):
    return pl.BlockSpec((sub, length), lambda step: (lax.rem(step + slots - back, slots), 0))


def call_params():
    return pltpu.CompilerParams(
        dimension_semantics=("arbitrary",), vmem_limit_bytes=56 * 1024 * 1024
    )


def run_forward(normed, weights, taps, cbc, head, seq_len, inner, state, kernel):
    rows, width = normed.shape[0], weights.shape[1]
    return pl.pallas_call(
        functools.partial(forward_kernel, inner=inner, state=state, kernel=kernel),
        grid=(rows // seq_len,),
        in_specs=[
            rows_spec(seq_len, normed.shape[1]),
            whole(weights),
            whole(taps),
            whole(cbc),
            whole(head),
        ],
        out_specs=[
            rows_spec(seq_len, width),
            rows_spec(seq_len, inner),
            rows_spec(seq_len, inner),
        ],
        out_shape=[
            jax.ShapeDtypeStruct((rows, width), f32),
            jax.ShapeDtypeStruct((rows, inner), f32),
            jax.ShapeDtypeStruct((rows, inner), f32),
        ],
        compiler_params=call_params(),
        name="mixer_forward",
    )(normed, weights, taps, cbc, head)


def run_gate(cot, out_full, gated, taps, seq_len, kernel):
    rows, inner = gated.shape
    slots = rows // seq_len
    return pl.pallas_call(
        functools.partial(gate_kernel, kernel=kernel),
        grid=(slots,),
        in_specs=[
            rows_spec(seq_len, cot.shape[1]),
            whole(out_full),
            rows_spec(seq_len, inner),
            whole(taps),
        ],
        out_specs=[
            rows_spec(seq_len, inner),
            rows_spec(sub, seq_len),
            rows_spec(seq_len, cot.shape[1]),
        ],
        out_shape=[
            jax.ShapeDtypeStruct((rows, inner), f32),
            jax.ShapeDtypeStruct((slots * sub, seq_len), f32),
            jax.ShapeDtypeStruct((rows, cot.shape[1]), bf16),
        ],
        compiler_params=call_params(),
        name="gate_products",
    )(cot, out_full, gated, taps)


def run_backward(stats, proj, plain, grad, taps, cbc, head, seq_len, inner, state, kernel, inner_all, turned):
    rows, width = proj.shape
    return pl.pallas_call(
        functools.partial(
            backward_kernel,
            inner=inner,
            state=state,
            kernel=kernel,
            inner_all=inner_all,
            stat_parts=len(stats),
        ),
        grid=(rows // seq_len,),
        in_specs=[stat_spec(seq_len, rows // seq_len, back if turned else 0) for back in range(len(stats))]
        + [
            rows_spec(seq_len, width),
            rows_spec(seq_len, inner),
            rows_spec(seq_len, inner),
            whole(taps),
            whole(cbc),
            whole(head),
        ],
        out_specs=[
            rows_spec(seq_len, width),
            rows_spec(seq_len, inner),
            pl.BlockSpec(taps.shape, lambda step: (0, 0)),
            pl.BlockSpec(cbc.shape, lambda step: (0, 0)),
            pl.BlockSpec(head.shape, lambda step: (0, 0)),
        ],
        out_shape=[
            jax.ShapeDtypeStruct((rows, width), bf16),
            jax.ShapeDtypeStruct((rows, inner), bf16),
            jax.ShapeDtypeStruct(taps.shape, f32),
            jax.ShapeDtypeStruct(cbc.shape, f32),
            jax.ShapeDtypeStruct(head.shape, f32),
        ],
        scratch_shapes=[pltpu.VMEM((seq_len, seq_len), f32)],
        compiler_params=call_params(),
        name="mixer_backward",
    )(*stats, proj, plain, grad, taps, cbc, head)


def adam_update(parameter, moments, gradient, learn_rate, decay_coef):
    first_mom = beta_one * moments[0] + (1.0 - beta_one) * gradient
    second_mom = beta_two * moments[1] * moments[1] + (1.0 - beta_two) * gradient * gradient
    second_root = jnp.sqrt(second_mom)
    first_hat = first_mom / (1.0 - beta_one**step_count)
    second_hat = second_mom / (1.0 - beta_two**step_count)
    updated = parameter - learn_rate * (
        first_hat / (jnp.sqrt(second_hat) + adam_eps) + decay_coef * parameter
    )
    return (updated, jnp.stack([first_mom, second_root]))


def shift_by(values, axis, count, amount):
    return lax.ppermute(values, axis, [(i, (i + amount) % count) for i in range(count)])


def swap_by(values, axis, count, mask):
    return lax.ppermute(values, axis, [(i, i ^ mask) for i in range(count)])


def pad_to(values, rows, cols):
    return jnp.pad(values, ((0, rows - values.shape[0]), (0, cols - values.shape[1])))


def gather_dp(piece, count):
    if count != 8:
        return lax.all_gather(piece, "dp", axis=0, tiled=True)
    rows = piece.shape[0]
    half = rows // 2
    place = lax.axis_index("dp")
    by_two = swap_by(piece, "dp", count, 2)
    by_four = swap_by(piece, "dp", count, 4)
    six_top = swap_by(by_two[:half], "dp", count, 4)
    six_low = swap_by(by_four[half:], "dp", count, 2)
    known = [(0, 0, piece), (2, 0, by_two), (4, 0, by_four), (6, 0, six_top), (6, half, six_low)]
    known = known + [
        (mask ^ 1, at, swap_by(values, "dp", count, 1)) for mask, at, values in known
    ]
    gathered = jnp.zeros((count * rows, piece.shape[1]), piece.dtype)
    for mask, at, values in known:
        gathered = lax.dynamic_update_slice(gathered, values, ((place ^ mask) * rows + at, 0))
    return gathered


def scatter_dp(full, count):
    if count != 8:
        return lax.psum_scatter(full, "dp", scatter_dimension=0, tiled=True).astype(f32)
    rows = full.shape[0] // count
    half = rows // 2
    place = lax.axis_index("dp")

    def piece(mask, start, size):
        return lax.dynamic_slice_in_dim(full, (place ^ mask) * rows + start, size, 0)

    def send(values, mask):
        return swap_by(values.astype(bf16), "dp", count, mask).astype(f32)

    def paired(mask, start, size):
        return piece(mask, start, size).astype(f32) + send(piece(mask ^ 1, start, size), 1)

    own = paired(0, 0, rows)
    six_top, six_low = paired(6, 0, half), paired(6, half, half)
    two_top, two_low = paired(2, 0, half), paired(2, half, half)
    four_top, four_low = paired(4, 0, half), paired(4, half, half)
    four_top = four_top + send(six_top, 2)
    two_low = two_low + send(six_low, 4)
    own_top = own[:half] + send(two_top, 2) + send(four_top, 4)
    own_low = own[half:] + send(two_low, 2) + send(four_low, 4)
    return jnp.concatenate([own_top, own_low], axis=0)


def sum_over(values, axis, count, keep_type=True):
    if count > 8:
        return lax.psum(values, axis)
    total = values
    for amount in range(1, count):
        total = total + shift_by(values, axis, count, amount)
    return total


def shards(
    block_input,
    seq_lengths,
    cotangent,
    norm_gain,
    proj_zx,
    proj_dt,
    proj_bc,
    chan_params,
    conv_bc,
    head_params,
    out_proj,
    gain_moments,
    zx_moments,
    dt_moments,
    bc_moments,
    chan_moments,
    convbc_moments,
    head_moments,
    out_moments,
):
    heads_axis = lax.axis_size("head")
    dp_axis = lax.axis_size("dp")
    slot_count = seq_lengths.shape[0]
    rows_own, model_width = block_input.shape
    rows_dev = rows_own * heads_axis
    seq_len = rows_dev // slot_count
    rows_dp = proj_zx.shape[0]
    inner = chan_params.shape[1]
    inner_all = inner * heads_axis
    heads_loc = head_params.shape[1]
    headdim = inner // heads_loc
    kernel = chan_params.shape[0] - 2
    state = conv_bc.shape[1] // 2
    place = lax.axis_index("head")
    whole_slots = rows_own == seq_len and heads_axis <= 4

    positions = iota((slot_count, seq_len), 1)
    live_mask = (positions < seq_lengths[:, None]).astype(f32).reshape(rows_dev, 1)
    live_own = lax.dynamic_slice_in_dim(live_mask, place * rows_own, rows_own, 0)
    gain_float = lax.optimization_barrier(norm_gain.astype(bf16)).astype(f32)
    input_float = block_input.astype(f32)
    inv_own = lax.rsqrt(jnp.mean(input_float * input_float, axis=-1, keepdims=True) + norm_eps)
    own_hat = input_float * inv_own
    normed_own = (own_hat * gain_float[None, :]).astype(bf16)
    cot_float = cotangent.astype(f32)
    cot_own = (cot_float * live_own).astype(bf16)

    def gather_head(own):
        if not whole_slots:
            return lax.all_gather(own, "head", axis=0, tiled=True)
        return jnp.concatenate(
            [own] + [shift_by(own, "head", heads_axis, k) for k in range(1, heads_axis)], axis=0
        )

    def scatter_head(full):
        if not whole_slots:
            return lax.psum_scatter(full, "head", scatter_dimension=0, tiled=True).astype(f32)
        total = full[:rows_own].astype(f32)
        for k in range(1, heads_axis):
            piece = full[k * rows_own : (k + 1) * rows_own]
            total = total + shift_by(piece, "head", heads_axis, heads_axis - k).astype(f32)
        return total

    piece_in = jnp.concatenate(
        [
            proj_zx.astype(bf16).reshape(rows_dp, 2 * inner),
            proj_bc.astype(bf16),
            pad_to(proj_dt.astype(bf16), rows_dp, lanes),
        ],
        axis=1,
    )
    normed_all = gather_head(normed_own)
    weights_in = gather_dp(piece_in, dp_axis)
    out_full = gather_dp(out_proj.astype(bf16), dp_axis)
    cot_all = gather_head(cot_own)

    taps = pad_to(
        jnp.concatenate([chan_params, jnp.repeat(head_params[2:3], headdim, axis=1)], axis=0),
        sub,
        inner,
    )
    cbc = pad_to(conv_bc, sub, 2 * state)
    head_table = pad_to(head_params, sub, lanes)

    proj, plain, gated = run_forward(
        normed_all, weights_in, taps, cbc, head_table, seq_len, inner, state, kernel
    )
    grad_normed, stats, branch = run_gate(cot_all, out_full, gated, taps, seq_len, kernel)
    if heads_axis <= 4:
        stat_parts = [stats] + [shift_by(stats, "head", heads_axis, k) for k in range(1, heads_axis)]
    else:
        stat_parts = [lax.psum(stats, "head")]
    cot_proj, normed_out, tap_sums, cbc_sums, head_sums = run_backward(
        stat_parts,
        proj,
        plain,
        grad_normed,
        taps,
        cbc,
        head_table,
        seq_len,
        inner,
        state,
        kernel,
        inner_all,
        whole_slots,
    )
    grad_out = dot(normed_out, cot_all, (0, 0)).astype(bf16)
    grad_in = dot(normed_all, cot_proj, (0, 0)).astype(bf16)
    cot_input = dot(cot_proj, weights_in, (1, 1))
    grad_gain = jnp.sum(cot_input * normed_all.astype(f32), axis=0)
    cot_input = cot_input.astype(bf16)

    if whole_slots:
        square_own = stat_parts[0][:1]
        for k in range(1, heads_axis):
            at = (heads_axis - k) * sub
            square_own = square_own + stat_parts[k][at : at + 1]
        gate_own = lax.rsqrt(square_own / inner_all + norm_eps).reshape(rows_own, 1)
    else:
        total = sum(stat_parts).reshape(slot_count, sub, seq_len)[:, 0].reshape(rows_dev, 1)
        gate_own = lax.rsqrt(
            lax.dynamic_slice_in_dim(total, place * rows_own, rows_own, 0) / inner_all + norm_eps
        )
    branch_own = scatter_head(branch) * gate_own
    block_output = (input_float + live_own * branch_own).astype(bf16)
    cot_whole = scatter_head(cot_input)
    lifted = cot_whole * gain_float[None, :]
    row_dot = jnp.sum(lifted * own_hat, axis=-1, keepdims=True)
    input_grad = cot_float + inv_own * (lifted - own_hat * row_dot / model_width)

    grad_out = scatter_dp(grad_out, dp_axis)
    grad_in = scatter_dp(grad_in, dp_axis)
    grad_zx = grad_in[:, : 2 * inner].reshape(rows_dp, 2, inner)
    grad_bc = grad_in[:, 2 * inner : 2 * inner + 2 * state]
    grad_dt = grad_in[:, 2 * inner + 2 * state :][:, :heads_loc]
    if heads_axis <= 4:
        grad_bc = grad_bc + sum(
            shift_by(grad_bc.astype(bf16), "head", heads_axis, k).astype(f32)
            for k in range(1, heads_axis)
        )
    else:
        grad_bc = lax.psum(grad_bc.astype(bf16), "head").astype(f32)

    both = jnp.concatenate([cbc_sums.reshape(-1, lanes), grad_gain.reshape(-1, lanes)], axis=0)
    both_rows = both.shape[0]
    small = jnp.concatenate([both, tap_sums.reshape(-1, lanes), head_sums], axis=0)
    small = sum_over(small, "dp", dp_axis)
    both = sum_over(small[:both_rows], "head", heads_axis)
    cbc_rows = sub * 2 * state // lanes
    grad_convbc = both[:cbc_rows].reshape(sub, 2 * state)[: kernel + 1]
    grad_gain = both[cbc_rows:].reshape(model_width) / gain_float
    tap_rows = sub * inner // lanes
    tap_sums = small[both_rows : both_rows + tap_rows].reshape(sub, inner)
    head_sums = small[both_rows + tap_rows :]
    grad_chan = tap_sums[: kernel + 2]
    grad_skip = jnp.sum(tap_sums[kernel + 2].reshape(heads_loc, headdim), axis=1)
    grad_head = jnp.concatenate([head_sums[:2, :heads_loc], grad_skip[None, :]], axis=0)

    gain_next, gain_state = adam_update(norm_gain, gain_moments, grad_gain, rate_vector, 0.0)
    zx_next, zx_state = adam_update(proj_zx, zx_moments, grad_zx, rate_matrix, weight_decay)
    dt_next, dt_state = adam_update(proj_dt, dt_moments, grad_dt, rate_matrix, weight_decay)
    bc_next, bc_state = adam_update(proj_bc, bc_moments, grad_bc, rate_matrix, weight_decay)
    chan_next, chan_state = adam_update(chan_params, chan_moments, grad_chan, rate_vector, 0.0)
    convbc_next, convbc_state = adam_update(conv_bc, convbc_moments, grad_convbc, rate_vector, 0.0)
    head_next, head_state = adam_update(head_params, head_moments, grad_head, rate_vector, 0.0)
    outproj_next, outproj_state = adam_update(
        out_proj, out_moments, grad_out, rate_matrix, weight_decay
    )
    return (
        block_output,
        input_grad,
        gain_next,
        gain_state,
        zx_next,
        zx_state,
        dt_next,
        dt_state,
        bc_next,
        bc_state,
        chan_next,
        chan_state,
        convbc_next,
        convbc_state,
        head_next,
        head_state,
        outproj_next,
        outproj_state,
    )


def solution(mesh):
    placed = (
        P(("dp", "head"), None),
        P("dp"),
        P(("dp", "head"), None),
        P(),
        P("dp", None, "head"),
        P("dp", "head"),
        P("dp", None),
        P(None, "head"),
        P(),
        P(None, "head"),
        P(("head", "dp"), None),
        P(),
        P(None, "dp", None, "head"),
        P(None, "dp", "head"),
        P(None, "dp", None),
        P(None, None, "head"),
        P(),
        P(None, None, "head"),
        P(None, ("head", "dp"), None),
    )
    return jax.shard_map(
        shards,
        mesh=mesh,
        in_specs=placed,
        out_specs=(
            P(("dp", "head"), None),
            P(("dp", "head"), None),
            P(),
            P(),
            P("dp", None, "head"),
            P(None, "dp", None, "head"),
            P("dp", "head"),
            P(None, "dp", "head"),
            P("dp", None),
            P(None, "dp", None),
            P(None, "head"),
            P(None, None, "head"),
            P(),
            P(),
            P(None, "head"),
            P(None, None, "head"),
            P(("head", "dp"), None),
            P(None, ("head", "dp"), None),
        ),
        check_vma=False,
    )
```

```python
import functools

import jax
import jax.numpy as jnp
from jax import lax
from jax.experimental import pallas as pl
from jax.experimental.pallas import tpu as pltpu
from jax.sharding import PartitionSpec as P

norm_eps = 1e-05
beta_one = 0.9
beta_two = 0.95
adam_eps = 1e-08
step_count = 3.0
rate_matrix = 0.005
rate_vector = 0.2
weight_decay = 0.1
lanes = 128
sub = 8
f32 = jnp.float32
bf16 = jnp.bfloat16


def dot(lhs, rhs, over=(1, 0)):
    return lax.dot_general(
        lhs, rhs, (((over[0],), (over[1],)), ((), ())), preferred_element_type=f32
    )


def dot_exact(lhs, rhs, over=(1, 0)):
    return lax.dot_general(
        lhs,
        rhs,
        (((over[0],), (over[1],)), ((), ())),
        precision=lax.Precision.HIGHEST,
        preferred_element_type=f32,
    )


def iota(shape, axis):
    return lax.broadcasted_iota(jnp.int32, shape, axis)


def later(values, count):
    if count == 0:
        return values
    rolled = pltpu.roll(values, count, 0)
    return jnp.where(iota(values.shape, 0) >= count, rolled, 0.0)


def earlier(values, count):
    if count == 0:
        return values
    length = values.shape[0]
    rolled = pltpu.roll(values, length - count, 0)
    return jnp.where(iota(values.shape, 0) < length - count, rolled, 0.0)


def conv(values, taps, kernel):
    summed = taps[kernel : kernel + 1] + taps[kernel - 1 : kernel] * values
    for offset in range(kernel - 1):
        summed = summed + taps[offset : offset + 1] * later(values, kernel - 1 - offset)
    return summed


def conv_back(grads, taps, kernel):
    summed = taps[kernel - 1 : kernel] * grads
    for offset in range(kernel - 1):
        summed = summed + taps[offset : offset + 1] * earlier(grads, kernel - 1 - offset)
    return summed


def conv_sums(grads, values, kernel):
    rows = [
        jnp.sum(grads * later(values, kernel - 1 - offset), axis=0, keepdims=True)
        for offset in range(kernel)
    ]
    rows.append(jnp.sum(grads, axis=0, keepdims=True))
    return rows


def sigmoid(values):
    return 1.0 / (1.0 + jnp.exp(-values))


def shared_parts(bc_rows, step_raw, cbc_ref, head_ref, state, kernel):
    step_raw = step_raw + head_ref[1:2, :]
    length = bc_rows.shape[0]
    bc_pre = conv(bc_rows, cbc_ref, kernel)
    bc_sig = sigmoid(bc_pre)
    shared = bc_pre * bc_sig
    step = jnp.maximum(step_raw, 0.0) + jnp.log1p(jnp.exp(-jnp.abs(step_raw)))
    rate = -jnp.exp(head_ref[0:1, :])
    lower = (iota((length, length), 0) >= iota((length, length), 1)).astype(f32)
    cum = dot_exact(lower, step * rate)
    in_map = shared[:, :state].astype(bf16)
    out_map = shared[:, state:].astype(bf16)
    scores = dot(out_map, in_map, (1, 1)) * lower
    return dict(
        bc_rows=bc_rows,
        bc_pre=bc_pre,
        bc_sig=bc_sig,
        step_raw=step_raw,
        step=step,
        rate=rate,
        cum=cum,
        cum_t=cum.T,
        in_map=in_map,
        out_map=out_map,
        scores=scores,
    )


def pick(values, pair, first):
    return jnp.where(
        first, values[:, 2 * pair : 2 * pair + 1], values[:, 2 * pair + 1 : 2 * pair + 2]
    )


def blocks_of(length):
    half = length // 2
    return [((0, half), (0, half)), ((half, length), (0, length))]


def place_pieces(place, pieces, target, sems):
    copies = []
    for at, (mask, ref) in enumerate(pieces):
        rows = ref.shape[0]
        start = pl.multiple_of((place ^ mask) * rows, 32)
        copies.append(
            pltpu.make_async_copy(ref, target.at[pl.ds(start, rows), :], sems.at[at])
        )
    for copy in copies:
        copy.start()
    return copies


piece_masks = (0, 2, 4, 6, 1, 3, 5, 7)


def forward_kernel(*refs, inner, state, kernel, split, primary):
    if split:
        place_ref, x_ref = refs[:2]
        pieces_a, pieces_b = refs[2:10], refs[10:18]
        rest = refs[18:]
    else:
        x_ref, wa_ref, wb_ref = refs[:3]
        rest = refs[3:]
    if not primary:
        bc_ref = rest[0]
        rest = rest[1:]
    taps_ref, cbc_ref, head_ref, proja_ref, projb_ref, y_ref, gated_ref = rest[:7]
    if split:
        wa_ref, wb_ref, sems = rest[7:]

        @pl.when(pl.program_id(0) == 0)
        def assemble():
            place = place_ref[0]
            copies = place_pieces(place, list(zip(piece_masks, pieces_a)), wa_ref, sems.at[0])
            copies = copies + place_pieces(
                place, list(zip(piece_masks, pieces_b)), wb_ref, sems.at[1]
            )
            for copy in copies:
                copy.wait()

    length = x_ref.shape[0]
    rows = x_ref[...]
    for weights, target in ((wa_ref, proja_ref), (wb_ref, projb_ref)):
        width = weights.shape[1]
        for start in range(0, width, 256):
            stop = min(width, start + 256)
            target[:, start:stop] = dot(rows, weights[:, start:stop])
    bc_rows = proja_ref[:, inner:] if primary else bc_ref[...]
    part = shared_parts(bc_rows, projb_ref[:, inner:], cbc_ref, head_ref, state, kernel)
    step, cum, cum_t, scores = part["step"], part["cum"], part["cum_t"], part["scores"]
    first = iota((length, lanes), 1) < lanes // 2
    for pair in range(inner // lanes):
        cols = slice(pair * lanes, (pair + 1) * lanes)
        taps = taps_ref[:, cols]
        gate = proja_ref[:, cols]
        values = conv(projb_ref[:, cols], taps, kernel)
        values = values * sigmoid(values)
        scaled = values * pick(step, pair, first)
        halves = (
            jnp.where(first, scaled, 0.0).astype(bf16),
            jnp.where(first, 0.0, scaled).astype(bf16),
        )
        pieces = []
        for (r0, r1), (c0, c1) in blocks_of(length):
            total = None
            for side in range(2):
                head = 2 * pair + side
                gap = cum[r0:r1, head : head + 1] - cum_t[head : head + 1, c0:c1]
                weights = (scores[r0:r1, c0:c1] * jnp.exp(jnp.minimum(gap, 0.0))).astype(bf16)
                term = dot(weights, halves[side][c0:c1])
                total = term if total is None else total + term
            pieces.append(total)
        output = jnp.concatenate(pieces, axis=0)
        y_ref[:, cols] = output
        gated_ref[:, cols] = (output + taps[kernel + 2 : kernel + 3] * values) * (
            gate * sigmoid(gate)
        )


def gate_kernel(*refs, kernel, split, blocks):
    if split:
        place_ref, cot_ref = refs[:2]
        pieces = [refs[2 + 8 * at : 10 + 8 * at] for at in range(blocks)]
        rest = refs[2 + 8 * blocks :]
    else:
        cot_ref = refs[0]
        out_refs = refs[1 : 1 + blocks]
        rest = refs[1 + blocks :]
    gated_refs, taps_refs = rest[:blocks], rest[blocks : 2 * blocks]
    grad_refs = rest[2 * blocks : 3 * blocks]
    stats_ref, branch_ref, lifted_ref = rest[3 * blocks : 3 * blocks + 3]
    if split:
        out_refs = rest[3 * blocks + 3 : 4 * blocks + 3]
        sems = rest[4 * blocks + 3]

        @pl.when(pl.program_id(0) == 0)
        def assemble():
            place = place_ref[0]
            copies = []
            for at in range(blocks):
                copies = copies + place_pieces(
                    place, list(zip(piece_masks, pieces[at])), out_refs[at], sems.at[at]
                )
            for copy in copies:
                copy.wait()

    cot = cot_ref[...]
    branch, squares, cross = None, None, None
    for at in range(blocks):
        gain = taps_refs[at][kernel + 1 : kernel + 2, :]
        weights = out_refs[at][...]
        grad = dot(cot, weights, (1, 1))
        grad_refs[at][...] = grad
        gated = gated_refs[at][...]
        inner = gated.shape[1]
        lifted = gated * gain
        low = lifted.astype(bf16)
        lifted_ref[:, at * inner : (at + 1) * inner] = low
        term = dot(low, weights)
        branch = term if branch is None else branch + term
        ones = jnp.ones((sub, inner), f32)
        term = dot_exact(ones, gated * gated, (1, 1))
        squares = term if squares is None else squares + term
        term = dot_exact(ones, grad * lifted, (1, 1))
        cross = term if cross is None else cross + term
    branch_ref[...] = branch.astype(bf16)
    stats_ref[...] = jnp.where(iota(squares.shape, 0) == 0, squares, cross)


def backward_kernel(*refs, inner, state, kernel, inner_all, stat_parts, primary, joined):
    stat_refs = refs[:stat_parts]
    proja_ref, projb_ref = refs[stat_parts : stat_parts + 2]
    rest = refs[stat_parts + 2 :]
    if not primary:
        bc_ref = rest[0]
        rest = rest[1:]
    if joined:
        joined_ref = rest[0]
        rest = rest[1:]
    y_ref, grad_ref, taps_ref, cbc_ref, head_ref, cota_ref, cotb_ref = rest[:7]
    tap_sums_ref, head_sums_ref = rest[7:9]
    bc_out_ref = rest[9]
    score_ref = rest[10]
    length = proja_ref.shape[0]
    half_lanes = lanes // 2

    @pl.when(pl.program_id(0) == 0)
    def clear():
        tap_sums_ref[...] = jnp.zeros(tap_sums_ref.shape, f32)
        head_sums_ref[...] = jnp.zeros(head_sums_ref.shape, f32)
        if primary:
            bc_out_ref[...] = jnp.zeros(bc_out_ref.shape, f32)

    stats = stat_refs[0][...]
    for more in stat_refs[1:]:
        stats = stats + more[...]
    unit = (iota((length, length), 0) == iota((length, length), 1)).astype(f32)
    columns = dot_exact(unit, stats, (1, 1))
    inv = lax.rsqrt(columns[:, 0:1] / inner_all + norm_eps)
    pull = inv * inv * inv * columns[:, 1:2] / inner_all

    bc_rows = proja_ref[:, inner:] if primary else bc_ref[...]
    part = shared_parts(bc_rows, projb_ref[:, inner:], cbc_ref, head_ref, state, kernel)
    step, cum, cum_t, scores = part["step"], part["cum"], part["cum_t"], part["scores"]
    first = iota((length, lanes), 1) < half_lanes
    score_ref[...] = jnp.zeros(score_ref.shape, f32)
    cum_grad = jnp.zeros((length, lanes), f32)
    step_grad = jnp.zeros((length, lanes), f32)
    for pair in range(inner // lanes):
        cols = slice(pair * lanes, (pair + 1) * lanes)
        taps = taps_ref[:, cols]
        gain = taps[kernel + 1 : kernel + 2]
        skip = taps[kernel + 2 : kernel + 3]
        gate = proja_ref[:, cols]
        raw = projb_ref[:, cols]
        pre = conv(raw, taps, kernel)
        pre_sig = sigmoid(pre)
        values = pre * pre_sig
        spread = pick(step, pair, first)
        scaled = values * spread
        gate_sig = sigmoid(gate)
        lift = gate * gate_sig
        plain = y_ref[:, cols]
        output = plain + skip * values
        gated = output * lift
        normed = gated * inv
        grad = grad_ref[:, cols]
        gain_row = jnp.sum(grad * normed, axis=0, keepdims=True)
        gated_grad = inv * (grad * gain) - gated * pull
        cota_ref[:, cols] = (
            gated_grad * output * (gate_sig * (1.0 + gate * (1.0 - gate_sig)))
        ).astype(bf16)
        out_grad = gated_grad * lift
        skip_row = jnp.sum(out_grad * values, axis=0, keepdims=True)
        out_low = out_grad.astype(bf16)
        scaled_low = scaled.astype(bf16)
        zero = jnp.zeros_like(out_low)
        sides = (jnp.where(first, out_low, zero), jnp.where(first, zero, out_low))
        half = length // 2
        pulled = [jnp.zeros((half, lanes), f32), jnp.zeros((half, lanes), f32)]
        for (r0, r1), (c0, c1) in blocks_of(length):
            score_sum = score_ref[r0:r1, c0:c1]
            for side in range(2):
                head = 2 * pair + side
                gap = cum[r0:r1, head : head + 1] - cum_t[head : head + 1, c0:c1]
                decay = jnp.exp(jnp.minimum(gap, 0.0))
                weights = (scores[r0:r1, c0:c1] * decay).astype(bf16)
                score_sum = score_sum + dot(sides[side][r0:r1], scaled_low[c0:c1], (1, 1)) * decay
                back = dot(weights, sides[side][r0:r1], (0, 0))
                pulled[0] = pulled[0] + back[:half]
                if c1 > half:
                    pulled[1] = pulled[1] + back[half:]
            score_ref[r0:r1, c0:c1] = score_sum
        scaled_grad = jnp.concatenate(pulled, axis=0)
        hot = (
            2 * pair + (iota((lanes, lanes), 0) >= half_lanes).astype(jnp.int32)
            == iota((lanes, lanes), 1)
        ).astype(f32)
        balance = out_low.astype(f32) * plain - scaled_low.astype(f32) * scaled_grad
        cum_grad = cum_grad + dot_exact(balance, hot)
        step_grad = step_grad + dot_exact(values * scaled_grad, hot)
        value_grad = skip * out_grad + scaled_grad * spread
        pre_grad = value_grad * (pre_sig * (1.0 + pre * (1.0 - pre_sig)))
        cotb_ref[:, cols] = conv_back(pre_grad, taps, kernel).astype(bf16)
        rows = conv_sums(pre_grad, raw, kernel) + [gain_row, skip_row]
        rows = rows + [jnp.zeros_like(gain_row)] * (tap_sums_ref.shape[0] - len(rows))
        tap_sums_ref[:, cols] = tap_sums_ref[:, cols] + jnp.concatenate(rows, axis=0)

    lower = iota((length, length), 0) >= iota((length, length), 1)
    score_low = jnp.where(lower, score_ref[...], 0.0).astype(bf16)
    shared_grad = jnp.concatenate(
        [dot(score_low, part["out_map"], (0, 0)), dot(score_low, part["in_map"])], axis=1
    )
    if joined:
        shared_grad = shared_grad + joined_ref[...]
    if primary:
        bc_pre, bc_sig = part["bc_pre"], part["bc_sig"]
        bc_grad = shared_grad * (bc_sig * (1.0 + bc_pre * (1.0 - bc_sig)))
        cota_ref[:, inner:] = conv_back(bc_grad, cbc_ref, kernel).astype(bf16)
        rows = conv_sums(bc_grad, part["bc_rows"], kernel)
        rows = rows + [jnp.zeros_like(rows[0])] * (bc_out_ref.shape[0] - len(rows))
        bc_out_ref[...] = bc_out_ref[...] + jnp.concatenate(rows, axis=0)
    else:
        bc_out_ref[...] = shared_grad
    decay_grad = dot_exact(lower.astype(f32), cum_grad, (0, 0))
    raw_grad = (step_grad + decay_grad * part["rate"]) * sigmoid(part["step_raw"])
    cotb_ref[:, inner:] = raw_grad.astype(bf16)
    rows = [
        part["rate"] * jnp.sum(step * decay_grad, axis=0, keepdims=True),
        jnp.sum(raw_grad, axis=0, keepdims=True),
    ]
    rows = rows + [jnp.zeros_like(rows[0])] * (head_sums_ref.shape[0] - len(rows))
    head_sums_ref[...] = head_sums_ref[...] + jnp.concatenate(rows, axis=0)


def product_kernel(place_ref, x_ref, grad_ref, keep_ref, send_ref, sum_ref, *, order):
    place = place_ref[0]
    rows = keep_ref.shape[1]
    sum_ref[...] = dot(x_ref[...], grad_ref[...], (0, 0))
    for at, mask in enumerate(order):
        start = pl.multiple_of((place ^ mask) * rows, 32)
        keep_ref[at] = sum_ref[pl.ds(start, rows), :].astype(bf16)
        start = pl.multiple_of((place ^ mask ^ 1) * rows, 32)
        send_ref[at] = sum_ref[pl.ds(start, rows), :].astype(bf16)


def whole(array):
    return pl.BlockSpec(array.shape, lambda step, *_: (0,) * array.ndim, pipeline_mode=pl.Buffered(1))


def rows_spec(length, width, column=0):
    return pl.BlockSpec((length, width), lambda step, *_: (step, column))


def fixed_spec(shape):
    return pl.BlockSpec(shape, lambda step, *_: (0,) * len(shape))


def any_spec():
    return pl.BlockSpec(memory_space=pl.ANY)


def stat_spec(length, slots, back):
    return pl.BlockSpec((sub, length), lambda step, *_: (lax.rem(step + slots - back, slots), 0))


def call_params():
    return pltpu.CompilerParams(
        dimension_semantics=("arbitrary",), vmem_limit_bytes=56 * 1024 * 1024
    )


def run_forward(place, normed, weights, bc_from, tables, seq_len, state, kernel):
    taps, cbc, head = tables
    rows, depth = normed.shape
    inner = taps.shape[1]
    split = isinstance(weights[0], (list, tuple))
    primary = bc_from is None
    if split:
        widths = [group[0].shape[1] for group in weights]
        prefix, ins = [place], [normed, *weights[0], *weights[1]]
        specs = [rows_spec(seq_len, depth)] + [any_spec()] * 16
    else:
        widths = [array.shape[1] for array in weights]
        prefix, ins = [], [normed, *weights]
        specs = [rows_spec(seq_len, depth)] + [whole(array) for array in weights]
    if not primary:
        ins.append(bc_from)
        specs.append(rows_spec(seq_len, 2 * state, inner // (2 * state)))
    for table in tables:
        ins.append(table)
        specs.append(whole(table))
    outs = [(widths[0], f32), (widths[1], f32), (inner, f32), (inner, f32)]
    out_specs = [rows_spec(seq_len, width) for width, _ in outs]
    out_shape = [jax.ShapeDtypeStruct((rows, width), kind) for width, kind in outs]
    scratch = []
    if split:
        out_specs = out_specs + [fixed_spec((depth, width)) for width in widths]
        out_shape = out_shape + [jax.ShapeDtypeStruct((depth, width), bf16) for width in widths]
        scratch = [pltpu.SemaphoreType.DMA((2, 8))]
    return pl.pallas_call(
        functools.partial(
            forward_kernel, inner=inner, state=state, kernel=kernel, split=split, primary=primary
        ),
        grid_spec=pltpu.PrefetchScalarGridSpec(
            num_scalar_prefetch=len(prefix),
            grid=(rows // seq_len,),
            in_specs=specs,
            out_specs=out_specs,
            scratch_shapes=scratch,
        ),
        out_shape=out_shape,
        compiler_params=call_params(),
        name="mixer_forward" if primary else "mixer_forward_more",
    )(*prefix, *ins)


def run_gate(place, cot, weights, gated, taps, seq_len, kernel):
    rows, inner = gated[0].shape
    slots, width = rows // seq_len, cot.shape[1]
    blocks = len(gated)
    split = isinstance(weights[0], (list, tuple))
    prefix, ins, specs, scratch = [], [cot], [rows_spec(seq_len, width)], []
    if split:
        prefix = [place]
        for group in weights:
            ins.extend(group)
            specs.extend([any_spec()] * 8)
        scratch = [pltpu.VMEM((inner, width), bf16)] * blocks + [
            pltpu.SemaphoreType.DMA((blocks, 8))
        ]
    else:
        ins.extend(weights)
        specs.extend([whole(array) for array in weights])
    ins.extend(gated)
    specs.extend([rows_spec(seq_len, inner)] * blocks)
    ins.extend(taps)
    specs.extend([whole(table) for table in taps])
    return pl.pallas_call(
        functools.partial(gate_kernel, kernel=kernel, split=split, blocks=blocks),
        grid_spec=pltpu.PrefetchScalarGridSpec(
            num_scalar_prefetch=len(prefix),
            grid=(slots,),
            in_specs=specs,
            out_specs=[rows_spec(seq_len, inner)] * blocks
            + [rows_spec(sub, seq_len), rows_spec(seq_len, width), rows_spec(seq_len, blocks * inner)],
            scratch_shapes=scratch,
        ),
        out_shape=[jax.ShapeDtypeStruct((rows, inner), f32)] * blocks
        + [
            jax.ShapeDtypeStruct((slots * sub, seq_len), f32),
            jax.ShapeDtypeStruct((rows, width), bf16),
            jax.ShapeDtypeStruct((rows, blocks * inner), bf16),
        ],
        compiler_params=call_params(),
        name="gate_products",
    )(*prefix, *ins)


def run_backward(stats, turned, proj, bc_from, joined, plain, grad, tables, seq_len, state, kernel, inner_all):
    taps, cbc, head = tables
    rows = plain.shape[0]
    inner = taps.shape[1]
    slots = rows // seq_len
    primary = bc_from is None
    ins = [*stats, *proj]
    specs = [stat_spec(seq_len, slots, back if turned else 0) for back in range(len(stats))]
    specs = specs + [rows_spec(seq_len, array.shape[1]) for array in proj]
    if not primary:
        ins.append(bc_from)
        specs.append(rows_spec(seq_len, 2 * state, inner // (2 * state)))
    if joined is not None:
        ins.append(joined)
        specs.append(rows_spec(seq_len, 2 * state))
    ins.extend([plain, grad])
    specs.extend([rows_spec(seq_len, inner)] * 2)
    for table in tables:
        ins.append(table)
        specs.append(whole(table))
    bc_shape = cbc.shape if primary else (rows, 2 * state)
    return pl.pallas_call(
        functools.partial(
            backward_kernel,
            inner=inner,
            state=state,
            kernel=kernel,
            inner_all=inner_all,
            stat_parts=len(stats),
            primary=primary,
            joined=joined is not None,
        ),
        grid=(slots,),
        in_specs=specs,
        out_specs=[
            rows_spec(seq_len, proj[0].shape[1]),
            rows_spec(seq_len, proj[1].shape[1]),
            fixed_spec(taps.shape),
            fixed_spec(head.shape),
            fixed_spec(cbc.shape) if primary else rows_spec(seq_len, 2 * state),
        ],
        out_shape=[
            jax.ShapeDtypeStruct((rows, proj[0].shape[1]), bf16),
            jax.ShapeDtypeStruct((rows, proj[1].shape[1]), bf16),
            jax.ShapeDtypeStruct(taps.shape, f32),
            jax.ShapeDtypeStruct(head.shape, f32),
            jax.ShapeDtypeStruct(bc_shape, f32),
        ],
        scratch_shapes=[pltpu.VMEM((seq_len, seq_len), f32)],
        compiler_params=call_params(),
        name="mixer_backward" if primary else "mixer_backward_more",
    )(*ins)


def run_product(place, x, grad, order, column=0, width=None):
    tokens = x.shape[0]
    depth = x.shape[1] if width is None else width
    cols = grad.shape[1]
    tile = 256 if cols % 256 == 0 else lanes
    rows = depth // 8
    block = pl.BlockSpec((4, rows, tile), lambda step, *_: (0, 0, step))
    return pl.pallas_call(
        functools.partial(product_kernel, order=order),
        grid_spec=pltpu.PrefetchScalarGridSpec(
            num_scalar_prefetch=1,
            grid=(cols // tile,),
            in_specs=[
                pl.BlockSpec(
                    (tokens, depth), lambda step, *_: (0, column), pipeline_mode=pl.Buffered(1)
                ),
                pl.BlockSpec((tokens, tile), lambda step, *_: (0, step)),
            ],
            out_specs=[block, block],
            scratch_shapes=[pltpu.VMEM((depth, tile), f32)],
        ),
        out_shape=[jax.ShapeDtypeStruct((4, rows, cols), bf16)] * 2,
        compiler_params=call_params(),
        name="weight_product",
    )(place, x, grad)


def adam_update(parameter, moments, gradient, learn_rate, decay_coef):
    first_mom = beta_one * moments[0] + (1.0 - beta_one) * gradient
    second_mom = beta_two * moments[1] * moments[1] + (1.0 - beta_two) * gradient * gradient
    second_root = jnp.sqrt(second_mom)
    first_hat = first_mom / (1.0 - beta_one**step_count)
    second_hat = second_mom / (1.0 - beta_two**step_count)
    updated = parameter - learn_rate * (
        first_hat / (jnp.sqrt(second_hat) + adam_eps) + decay_coef * parameter
    )
    return (updated, jnp.stack([first_mom, second_root]))


def swap_by(values, axis, count, mask):
    return lax.ppermute(values, axis, [(i, i ^ mask) for i in range(count)])


def pad_to(values, rows, cols):
    return jnp.pad(values, ((0, rows - values.shape[0]), (0, cols - values.shape[1])))


def gather_plane(piece, way):
    other = 6 - way
    near = swap_by(piece, "dp", 8, way)
    side = swap_by(piece, "dp", 8, other)
    far = swap_by(near, "dp", 8, other)
    mine = [piece, near, side, far] if way == 2 else [piece, side, near, far]
    return mine + [swap_by(values, "dp", 8, 1) for values in mine]


def order_of(way):
    return (0, 6 - way, way, 6)


def scatter_plane(keep, send, way):
    other = 6 - way
    got = swap_by(send, "dp", 8, 1)
    away = (keep[2:].astype(f32) + got[2:].astype(f32)).astype(bf16)
    near = swap_by(away, "dp", 8, way)
    here = keep[:2].astype(f32) + got[:2].astype(f32) + near.astype(f32)
    last = swap_by(here[1].astype(bf16), "dp", 8, other)
    return here[0] + last.astype(f32)


def sum_over(values, axis, count):
    if count & (count - 1):
        return lax.psum(values, axis)
    mask = 1
    while mask < count:
        values = values + swap_by(values, axis, count, mask)
        mask = mask * 2
    return values


def shards(
    block_input,
    seq_lengths,
    cotangent,
    norm_gain,
    proj_zx,
    proj_dt,
    proj_bc,
    chan_params,
    conv_bc,
    head_params,
    out_proj,
    gain_moments,
    zx_moments,
    dt_moments,
    bc_moments,
    chan_moments,
    convbc_moments,
    head_moments,
    out_moments,
):
    heads_axis = lax.axis_size("head")
    dp_axis = lax.axis_size("dp")
    slot_count = seq_lengths.shape[0]
    rows_own, model_width = block_input.shape
    rows_dev = rows_own * heads_axis
    seq_len = rows_dev // slot_count
    rows_dp = proj_zx.shape[0]
    inner = chan_params.shape[1]
    inner_all = inner * heads_axis
    heads_loc = head_params.shape[1]
    headdim = inner // heads_loc
    kernel = chan_params.shape[0] - 2
    state = conv_bc.shape[1] // 2
    spot = lax.axis_index("head")
    place = lax.axis_index("dp").astype(jnp.int32).reshape(1)
    paired = heads_axis == 4 and dp_axis == 8 and rows_own == seq_len

    zx_low = proj_zx.astype(bf16)
    piece_a = jnp.concatenate([zx_low[:, 0], proj_bc.astype(bf16)], axis=1)
    piece_b = jnp.concatenate([zx_low[:, 1], pad_to(proj_dt.astype(bf16), rows_dp, lanes)], axis=1)
    out_low = out_proj.astype(bf16)
    taps = pad_to(
        jnp.concatenate([chan_params, jnp.repeat(head_params[2:3], headdim, axis=1)], axis=0),
        sub,
        inner,
    )
    cbc = pad_to(conv_bc, sub, 2 * state)
    head_table = pad_to(head_params, sub, lanes)

    positions = iota((slot_count, seq_len), 1)
    live_mask = (positions < seq_lengths[:, None]).astype(f32).reshape(rows_dev, 1)
    live_own = lax.dynamic_slice_in_dim(live_mask, spot * rows_own, rows_own, 0)
    gain_float = lax.optimization_barrier(norm_gain.astype(bf16)).astype(f32)
    input_float = block_input.astype(f32)
    inv_own = lax.rsqrt(jnp.mean(input_float * input_float, axis=-1, keepdims=True) + norm_eps)
    own_hat = input_float * inv_own
    normed_own = (own_hat * gain_float[None, :]).astype(bf16)
    cot_float = cotangent.astype(f32)
    cot_own = (cot_float * live_own).astype(bf16)
    tables = (taps, cbc, head_table)

    if paired:
        more = swap_by(jnp.concatenate([zx_low[:, 0], piece_b], axis=1), "head", 4, 2)
        wide = jnp.concatenate([taps, head_table], axis=1)
        more_tables = swap_by(wide, "head", 4, 2)
        tables_more = (more_tables[:, :inner], cbc, more_tables[:, inner:])
        own_pieces = (gather_plane(piece_a, 2), gather_plane(piece_b, 4))
        normed_all = jnp.concatenate([normed_own, swap_by(normed_own, "head", 4, 1)], axis=0)
        more_pieces = (gather_plane(more[:, :inner], 2), gather_plane(more[:, inner:], 4))
        cot_all = jnp.concatenate([cot_own, swap_by(cot_own, "head", 4, 1)], axis=0)
        out_pieces = (
            gather_plane(out_low, 2),
            gather_plane(swap_by(out_low, "head", 4, 2), 4),
        )
        proj_a, proj_b, plain, gated, own_a, own_b = run_forward(
            place, normed_all, own_pieces, None, tables, seq_len, state, kernel
        )
        more_proj_a, more_proj_b, more_plain, more_gated, more_a, more_b = run_forward(
            place, normed_all, more_pieces, proj_a, tables_more, seq_len, state, kernel
        )
        grad, more_grad, stats, branch, lifted = run_gate(
            place,
            cot_all,
            out_pieces,
            (gated, more_gated),
            (taps, tables_more[0]),
            seq_len,
            kernel,
        )
        stat_parts = [stats, swap_by(stats, "head", 4, 1)]
        whole_stats = stats[:sub] + stat_parts[1][sub:], stats[sub:] + stat_parts[1][:sub]
        gate_rows = [
            lax.rsqrt(part[:1] / inner_all + norm_eps).reshape(seq_len, 1) for part in whole_stats
        ]
        gate_own = gate_rows[0]
        cot_gate = (cot_all.astype(f32) * jnp.concatenate(gate_rows, axis=0)).astype(bf16)
        out_own = run_product(place, lifted, cot_gate, order_of(2), 0, inner)
        out_more = run_product(place, lifted, cot_gate, order_of(4), 1, inner)
        more_cot_a, more_cot_b, more_tap_sums, more_head_sums, bc_part = run_backward(
            stat_parts,
            True,
            (more_proj_a, more_proj_b),
            proj_a,
            None,
            more_plain,
            more_grad,
            tables_more,
            seq_len,
            state,
            kernel,
            inner_all,
        )
        grad_more_a = run_product(place, normed_all, more_cot_a, order_of(2))
        grad_more_b = run_product(place, normed_all, more_cot_b, order_of(4))
        cot_a, cot_b, tap_sums, head_sums, cbc_sums = run_backward(
            stat_parts,
            True,
            (proj_a, proj_b),
            None,
            bc_part,
            plain,
            grad,
            tables,
            seq_len,
            state,
            kernel,
            inner_all,
        )
        grad_own_a = run_product(place, normed_all, cot_a, order_of(2))
        grad_own_b = run_product(place, normed_all, cot_b, order_of(4))
        cot_input = (
            dot(more_cot_a, more_a, (1, 1))
            + dot(more_cot_b, more_b, (1, 1))
            + dot(cot_a, own_a, (1, 1))
            + dot(cot_b, own_b, (1, 1))
        )
        grad_gain = jnp.sum(cot_input * normed_all.astype(f32), axis=0)
        cot_input = cot_input.astype(bf16)
        cot_whole = cot_input[:rows_own].astype(f32) + swap_by(
            cot_input[rows_own:], "head", 4, 1
        ).astype(f32)
        branch_own = branch[:rows_own].astype(f32) + swap_by(
            branch[rows_own:], "head", 4, 1
        ).astype(f32)
        out_sum = scatter_plane(*out_own, 2)
        out_sum = out_sum + swap_by(
            scatter_plane(*out_more, 4).astype(bf16), "head", 4, 2
        ).astype(f32)
        away = jnp.concatenate(
            [scatter_plane(*grad_more_a, 2), scatter_plane(*grad_more_b, 4)], axis=1
        ).astype(bf16)
        home = swap_by(away, "head", 4, 2).astype(f32)
        sum_a = scatter_plane(*grad_own_a, 2)
        sum_b = scatter_plane(*grad_own_b, 4)
        grad_out = out_sum
        grad_zx = jnp.stack(
            [sum_a[:, :inner] + home[:, :inner], sum_b[:, :inner] + home[:, inner : 2 * inner]],
            axis=1,
        )
        grad_dt = (sum_b[:, inner:] + home[:, 2 * inner :])[:, :heads_loc]
        grad_bc = sum_a[:, inner:]
        grad_bc = grad_bc + swap_by(grad_bc.astype(bf16), "head", 4, 1).astype(f32)
        grad_bc = grad_bc + swap_by(grad_bc.astype(bf16), "head", 4, 2).astype(f32)
        packs = [(more_tap_sums, more_head_sums), (tap_sums, head_sums)]
    else:
        normed_all = lax.all_gather(normed_own, "head", axis=0, tiled=True)
        cot_all = lax.all_gather(cot_own, "head", axis=0, tiled=True)
        own_a = lax.all_gather(piece_a, "dp", axis=0, tiled=True)
        own_b = lax.all_gather(piece_b, "dp", axis=0, tiled=True)
        out_full = lax.all_gather(out_low, "dp", axis=0, tiled=True)
        proj_a, proj_b, plain, gated = run_forward(
            None, normed_all, (own_a, own_b), None, tables, seq_len, state, kernel
        )
        grad, stats, branch, lifted = run_gate(
            None, cot_all, (out_full,), (gated,), (taps,), seq_len, kernel
        )
        stats = lax.psum(stats, "head")
        square = stats.reshape(slot_count, sub, seq_len)[:, 0].reshape(rows_dev, 1)
        gate_all = lax.rsqrt(square / inner_all + norm_eps)
        gate_own = lax.dynamic_slice_in_dim(gate_all, spot * rows_own, rows_own, 0)
        cot_gate = (cot_all.astype(f32) * gate_all).astype(bf16)
        cot_a, cot_b, tap_sums, head_sums, cbc_sums = run_backward(
            [stats],
            False,
            (proj_a, proj_b),
            None,
            None,
            plain,
            grad,
            tables,
            seq_len,
            state,
            kernel,
            inner_all,
        )
        cot_input = dot(cot_a, own_a, (1, 1)) + dot(cot_b, own_b, (1, 1))
        grad_gain = jnp.sum(cot_input * normed_all.astype(f32), axis=0)

        def scatter(values, axis):
            return lax.psum_scatter(
                values.astype(bf16), axis, scatter_dimension=0, tiled=True
            ).astype(f32)

        cot_whole = scatter(cot_input, "head")
        branch_own = scatter(branch, "head")
        grad_out = scatter(dot(lifted, cot_gate, (0, 0)), "dp")
        sum_a = scatter(dot(normed_all, cot_a, (0, 0)), "dp")
        sum_b = scatter(dot(normed_all, cot_b, (0, 0)), "dp")
        grad_zx = jnp.stack([sum_a[:, :inner], sum_b[:, :inner]], axis=1)
        grad_dt = sum_b[:, inner:][:, :heads_loc]
        grad_bc = lax.psum(sum_a[:, inner:].astype(bf16), "head").astype(f32)
        packs = [(tap_sums, head_sums)]

    block_output = (input_float + live_own * (branch_own * gate_own)).astype(bf16)
    lift_own = cot_whole * gain_float[None, :]
    row_dot = jnp.sum(lift_own * own_hat, axis=-1, keepdims=True)
    input_grad = cot_float + inv_own * (lift_own - own_hat * row_dot / model_width)

    parts = [cbc_sums.reshape(-1, lanes), grad_gain.reshape(-1, lanes)]
    both_rows = sum(part.shape[0] for part in parts)
    parts = parts + [jnp.concatenate(pack, axis=1).reshape(-1, lanes) for pack in packs]
    small = sum_over(jnp.concatenate(parts, axis=0), "dp", dp_axis)
    both = sum_over(small[:both_rows], "head", heads_axis)
    cbc_rows = sub * 2 * state // lanes
    grad_convbc = both[:cbc_rows].reshape(sub, 2 * state)[: kernel + 1]
    grad_gain = both[cbc_rows:].reshape(model_width) / gain_float
    pack_rows = sub * (inner + lanes) // lanes
    own_sums = small[small.shape[0] - pack_rows :]
    if paired:
        own_sums = own_sums + swap_by(small[both_rows : both_rows + pack_rows], "head", 4, 2)
    own_sums = own_sums.reshape(sub, inner + lanes)
    grad_chan = own_sums[: kernel + 2, :inner]
    grad_skip = jnp.sum(own_sums[kernel + 2, :inner].reshape(heads_loc, headdim), axis=1)
    grad_head = jnp.concatenate(
        [own_sums[:2, inner : inner + heads_loc], grad_skip[None, :]], axis=0
    )

    gain_next, gain_state = adam_update(norm_gain, gain_moments, grad_gain, rate_vector, 0.0)
    zx_next, zx_state = adam_update(proj_zx, zx_moments, grad_zx, rate_matrix, weight_decay)
    dt_next, dt_state = adam_update(proj_dt, dt_moments, grad_dt, rate_matrix, weight_decay)
    bc_next, bc_state = adam_update(proj_bc, bc_moments, grad_bc, rate_matrix, weight_decay)
    chan_next, chan_state = adam_update(chan_params, chan_moments, grad_chan, rate_vector, 0.0)
    convbc_next, convbc_state = adam_update(conv_bc, convbc_moments, grad_convbc, rate_vector, 0.0)
    head_next, head_state = adam_update(head_params, head_moments, grad_head, rate_vector, 0.0)
    outproj_next, outproj_state = adam_update(
        out_proj, out_moments, grad_out, rate_matrix, weight_decay
    )
    return (
        block_output,
        input_grad,
        gain_next,
        gain_state,
        zx_next,
        zx_state,
        dt_next,
        dt_state,
        bc_next,
        bc_state,
        chan_next,
        chan_state,
        convbc_next,
        convbc_state,
        head_next,
        head_state,
        outproj_next,
        outproj_state,
    )


def solution(mesh):
    placed = (
        P(("dp", "head"), None),
        P("dp"),
        P(("dp", "head"), None),
        P(),
        P("dp", None, "head"),
        P("dp", "head"),
        P("dp", None),
        P(None, "head"),
        P(),
        P(None, "head"),
        P(("head", "dp"), None),
        P(),
        P(None, "dp", None, "head"),
        P(None, "dp", "head"),
        P(None, "dp", None),
        P(None, None, "head"),
        P(),
        P(None, None, "head"),
        P(None, ("head", "dp"), None),
    )
    return jax.shard_map(
        shards,
        mesh=mesh,
        in_specs=placed,
        out_specs=(
            P(("dp", "head"), None),
            P(("dp", "head"), None),
            P(),
            P(),
            P("dp", None, "head"),
            P(None, "dp", None, "head"),
            P("dp", "head"),
            P(None, "dp", "head"),
            P("dp", None),
            P(None, "dp", None),
            P(None, "head"),
            P(None, None, "head"),
            P(),
            P(),
            P(None, "head"),
            P(None, None, "head"),
            P(("head", "dp"), None),
            P(None, ("head", "dp"), None),
        ),
        check_vma=False,
    )
```

```python
import functools
from types import SimpleNamespace

import jax
import jax.numpy as jnp
from jax import lax
from jax.experimental import pallas as pl
from jax.experimental.pallas import tpu as pltpu
from jax.sharding import PartitionSpec as P


norm_eps = 1e-05
beta_one = 0.9
beta_two = 0.95
adam_eps = 1e-08
step_count = 3.0
rate_matrix = 0.005
rate_vector = 0.2
weight_decay = 0.1
lanes = 128
HEAD = "head"
DP = "dp"
sub = 8
f32 = jnp.float32
bf16 = jnp.bfloat16


def dot(lhs, rhs, over=(1, 0)):
    return lax.dot_general(
        lhs, rhs, (((over[0],), (over[1],)), ((), ())), preferred_element_type=f32
    )


def dot_exact(lhs, rhs, over=(1, 0)):
    return lax.dot_general(
        lhs,
        rhs,
        (((over[0],), (over[1],)), ((), ())),
        precision=lax.Precision.HIGHEST,
        preferred_element_type=f32,
    )


def iota(shape, axis):
    return lax.broadcasted_iota(jnp.int32, shape, axis)


def later(values, count):
    if count == 0:
        return values
    rolled = pltpu.roll(values, count, 0)
    return jnp.where(iota(values.shape, 0) >= count, rolled, 0.0)


def earlier(values, count):
    if count == 0:
        return values
    length = values.shape[0]
    rolled = pltpu.roll(values, length - count, 0)
    return jnp.where(iota(values.shape, 0) < length - count, rolled, 0.0)


def conv(values, taps, kernel):
    summed = taps[kernel : kernel + 1] + taps[kernel - 1 : kernel] * values
    for offset in range(kernel - 1):
        summed = summed + taps[offset : offset + 1] * later(values, kernel - 1 - offset)
    return summed


def conv_back(grads, taps, kernel):
    summed = taps[kernel - 1 : kernel] * grads
    for offset in range(kernel - 1):
        summed = summed + taps[offset : offset + 1] * earlier(grads, kernel - 1 - offset)
    return summed


def conv_sums(grads, values, kernel):
    rows = [
        jnp.sum(grads * later(values, kernel - 1 - offset), axis=0, keepdims=True)
        for offset in range(kernel)
    ]
    rows.append(jnp.sum(grads, axis=0, keepdims=True))
    return rows


def sigmoid(values):
    return 1.0 / (1.0 + jnp.exp(-values))


def shared_parts(bc_rows, step_raw, cbc_ref, head_ref, state, kernel):
    step_raw = step_raw + head_ref[1:2, :]
    length = bc_rows.shape[0]
    bc_pre = conv(bc_rows, cbc_ref, kernel)
    bc_sig = sigmoid(bc_pre)
    shared = bc_pre * bc_sig
    step = jnp.maximum(step_raw, 0.0) + jnp.log1p(jnp.exp(-jnp.abs(step_raw)))
    rate = -jnp.exp(head_ref[0:1, :])
    lower = (iota((length, length), 0) >= iota((length, length), 1)).astype(f32)
    cum = dot_exact(lower, step * rate)
    in_map = shared[:, :state].astype(bf16)
    out_map = shared[:, state:].astype(bf16)
    scores = dot(out_map, in_map, (1, 1)) * lower
    return SimpleNamespace(
        bc_rows=bc_rows,
        bc_pre=bc_pre,
        bc_sig=bc_sig,
        step_raw=step_raw,
        step=step,
        rate=rate,
        cum=cum,
        cum_t=cum.T,
        in_map=in_map,
        out_map=out_map,
        scores=scores,
    )


def pick(values, pair, first):
    return jnp.where(
        first, values[:, 2 * pair : 2 * pair + 1], values[:, 2 * pair + 1 : 2 * pair + 2]
    )


def blocks_of(length):
    half = length // 2
    return [((0, half), (0, half)), ((half, length), (0, length))]


def place_pieces(place, pieces, target, sems):
    copies = []
    for at, (mask, ref) in enumerate(pieces):
        rows = ref.shape[0]
        start = pl.multiple_of((place ^ mask) * rows, 32)
        copies.append(
            pltpu.make_async_copy(ref, target.at[pl.ds(start, rows), :], sems.at[at])
        )
    for copy in copies:
        copy.start()
    return copies


piece_masks = (0, 2, 4, 6, 1, 3, 5, 7)


def forward_kernel(*refs, inner, state, kernel, split, primary):
    if split:
        place_ref, x_ref, peer_ref = refs[:3]
        pieces_a, pieces_b = refs[3:11], refs[11:19]
        rest = refs[19:]
    else:
        x_ref, wa_ref, wb_ref = refs[:3]
        rest = refs[3:]
    if not primary:
        bc_ref = rest[0]
        rest = rest[1:]
    taps_ref, cbc_ref, proja_ref, projb_ref, y_ref, gated_ref = rest[:6]
    head_ref = taps_ref.at[:, pl.ds(inner, lanes)]
    if split:
        wa_ref, wb_ref = rest[6:8]
        sems = rest[-1]

        @pl.when(pl.program_id(0) == 0)
        def assemble():
            place = place_ref[0]
            copies = place_pieces(place, list(zip(piece_masks, pieces_a)), wa_ref, sems.at[0])
            copies = copies + place_pieces(
                place, list(zip(piece_masks, pieces_b)), wb_ref, sems.at[1]
            )
            for copy in copies:
                copy.wait()

    length = x_ref.shape[0]
    rows = x_ref[...]
    if split:
        rows = jnp.where(pl.program_id(0) == 0, rows, peer_ref[...])
        if primary:
            turned_ref = rest[8]
            for start in range(0, rows.shape[1], lanes):
                turned_ref[start : start + lanes, :] = (
                    rows[:, start : start + lanes].astype(f32).T.astype(bf16)
                )
    for weights, target in ((wa_ref, proja_ref), (wb_ref, projb_ref)):
        width = weights.shape[1]
        for start in range(0, width, 256):
            stop = min(width, start + 256)
            target[:, start:stop] = dot(rows, weights[:, start:stop])
    bc_rows = proja_ref[:, inner:] if primary else bc_ref[...]
    part = shared_parts(bc_rows, projb_ref[:, inner:], cbc_ref, head_ref, state, kernel)
    step, cum, cum_t, scores = part.step, part.cum, part.cum_t, part.scores
    first = iota((length, lanes), 1) < lanes // 2
    for pair in range(inner // lanes):
        cols = slice(pair * lanes, (pair + 1) * lanes)
        taps = taps_ref[:, cols]
        gate = proja_ref[:, cols]
        values = conv(projb_ref[:, cols], taps, kernel)
        values = values * sigmoid(values)
        scaled = values * pick(step, pair, first)
        halves = (
            jnp.where(first, scaled, 0.0).astype(bf16),
            jnp.where(first, 0.0, scaled).astype(bf16),
        )
        pieces = []
        for (r0, r1), (c0, c1) in blocks_of(length):
            total = None
            for side in range(2):
                head = 2 * pair + side
                gap = cum[r0:r1, head : head + 1] - cum_t[head : head + 1, c0:c1]
                weights = (scores[r0:r1, c0:c1] * jnp.exp(jnp.minimum(gap, 0.0))).astype(bf16)
                term = dot(weights, halves[side][c0:c1])
                total = term if total is None else total + term
            pieces.append(total)
        output = jnp.concatenate(pieces, axis=0)
        y_ref[:, cols] = output
        gated_ref[:, cols] = (output + taps[kernel + 2 : kernel + 3] * values) * (
            gate * sigmoid(gate)
        )


def gate_kernel(*refs, kernel, split, blocks):
    if split:
        place_ref, cot_ref, peer_ref = refs[:3]
        pieces = [refs[3 + 8 * at : 11 + 8 * at] for at in range(blocks)]
        rest = refs[3 + 8 * blocks :]
    else:
        cot_ref = refs[0]
        out_refs = refs[1 : 1 + blocks]
        rest = refs[1 + blocks :]
    gated_refs, taps_refs = rest[:blocks], rest[blocks : 2 * blocks]
    grad_refs = rest[2 * blocks : 3 * blocks]
    stats_ref, turned_ref = rest[3 * blocks : 3 * blocks + 2]
    rest = rest[3 * blocks + 2 :]
    lifted_refs = rest[:blocks]
    if split:
        out_refs = rest[blocks : 2 * blocks]
        sems = rest[2 * blocks]

        @pl.when(pl.program_id(0) == 0)
        def assemble():
            place = place_ref[0]
            copies = []
            for at in range(blocks):
                copies = copies + place_pieces(
                    place, list(zip(piece_masks, pieces[at])), out_refs[at], sems.at[at]
                )
            for copy in copies:
                copy.wait()

    cot = cot_ref[...]
    if split:
        cot = jnp.where(pl.program_id(0) == 0, cot, peer_ref[...])
    squares, cross = None, None
    for at in range(blocks):
        grad = dot(cot, out_refs[at][...], (1, 1))
        grad_refs[at][...] = grad
        inner = grad.shape[1]
        for start in range(0, inner, lanes):
            cols = slice(start, start + lanes)
            gated = gated_refs[at][:, cols]
            lifted = gated * taps_refs[at][kernel + 1 : kernel + 2, cols]
            lifted_refs[at][:, cols] = lifted.astype(bf16)
            turned_ref[at * inner + start : at * inner + start + lanes, :] = lifted.T.astype(bf16)
            square, product = gated * gated, grad[:, cols] * lifted
            squares = square if squares is None else squares + square
            cross = product if cross is None else cross + product
    ones = jnp.ones((sub, lanes), f32)
    squares = dot_exact(ones, squares, (1, 1))
    cross = dot_exact(ones, cross, (1, 1))
    stats_ref[...] = jnp.where(iota(squares.shape, 0) == 0, squares, cross)


def backward_kernel(*refs, inner, state, kernel, inner_all, stat_parts, primary, joined):
    stat_refs = refs[:stat_parts]
    proja_ref, projb_ref = refs[stat_parts : stat_parts + 2]
    rest = refs[stat_parts + 2 :]
    if not primary:
        bc_ref = rest[0]
        rest = rest[1:]
    if joined:
        joined_ref = rest[0]
        rest = rest[1:]
    y_ref, grad_ref, taps_ref, cbc_ref, cota_ref, cotb_ref, tap_sums_ref = rest[:7]
    bc_out_ref, score_ref = rest[7:9]
    head_ref = taps_ref.at[:, pl.ds(inner, lanes)]
    length = proja_ref.shape[0]
    half_lanes = lanes // 2

    @pl.when(pl.program_id(0) == 0)
    def clear():
        tap_sums_ref[...] = jnp.zeros(tap_sums_ref.shape, f32)
        if primary:
            bc_out_ref[...] = jnp.zeros(bc_out_ref.shape, f32)

    stats = stat_refs[0][...]
    for more in stat_refs[1:]:
        stats = stats + more[...]
    unit = (iota((length, length), 0) == iota((length, length), 1)).astype(f32)
    columns = dot_exact(unit, stats, (1, 1))
    inv = lax.rsqrt(columns[:, 0:1] / inner_all + norm_eps)
    pull = inv * inv * inv * columns[:, 1:2] / inner_all

    bc_rows = proja_ref[:, inner:] if primary else bc_ref[...]
    part = shared_parts(bc_rows, projb_ref[:, inner:], cbc_ref, head_ref, state, kernel)
    step, cum, cum_t, scores = part.step, part.cum, part.cum_t, part.scores
    first = iota((length, lanes), 1) < half_lanes
    score_ref[...] = jnp.zeros(score_ref.shape, f32)
    cum_grad = jnp.zeros((length, lanes), f32)
    step_grad = jnp.zeros((length, lanes), f32)
    for pair in range(inner // lanes):
        cols = slice(pair * lanes, (pair + 1) * lanes)
        taps = taps_ref[:, cols]
        gain = taps[kernel + 1 : kernel + 2]
        skip = taps[kernel + 2 : kernel + 3]
        gate = proja_ref[:, cols]
        raw = projb_ref[:, cols]
        pre = conv(raw, taps, kernel)
        pre_sig = sigmoid(pre)
        values = pre * pre_sig
        spread = pick(step, pair, first)
        scaled = values * spread
        gate_sig = sigmoid(gate)
        lift = gate * gate_sig
        plain = y_ref[:, cols]
        output = plain + skip * values
        gated = output * lift
        normed = gated * inv
        grad = grad_ref[:, cols]
        gain_row = jnp.sum(grad * normed, axis=0, keepdims=True)
        gated_grad = inv * (grad * gain) - gated * pull
        cota_ref[:, cols] = (
            gated_grad * output * (gate_sig * (1.0 + gate * (1.0 - gate_sig)))
        ).astype(bf16)
        out_grad = gated_grad * lift
        skip_row = jnp.sum(out_grad * values, axis=0, keepdims=True)
        out_low = out_grad.astype(bf16)
        scaled_low = scaled.astype(bf16)
        zero = jnp.zeros_like(out_low)
        sides = (jnp.where(first, out_low, zero), jnp.where(first, zero, out_low))
        half = length // 2
        pulled = [jnp.zeros((half, lanes), f32), jnp.zeros((half, lanes), f32)]
        for (r0, r1), (c0, c1) in blocks_of(length):
            score_sum = score_ref[r0:r1, c0:c1]
            for side in range(2):
                head = 2 * pair + side
                gap = cum[r0:r1, head : head + 1] - cum_t[head : head + 1, c0:c1]
                decay = jnp.exp(jnp.minimum(gap, 0.0))
                weights = (scores[r0:r1, c0:c1] * decay).astype(bf16)
                score_sum = score_sum + dot(sides[side][r0:r1], scaled_low[c0:c1], (1, 1)) * decay
                back = dot(weights, sides[side][r0:r1], (0, 0))
                pulled[0] = pulled[0] + back[:half]
                if c1 > half:
                    pulled[1] = pulled[1] + back[half:]
            score_ref[r0:r1, c0:c1] = score_sum
        scaled_grad = jnp.concatenate(pulled, axis=0)
        hot = (
            2 * pair + (iota((lanes, lanes), 0) >= half_lanes).astype(jnp.int32)
            == iota((lanes, lanes), 1)
        ).astype(f32)
        balance = out_low.astype(f32) * plain - scaled_low.astype(f32) * scaled_grad
        cum_grad = cum_grad + dot_exact(balance, hot)
        step_grad = step_grad + dot_exact(values * scaled_grad, hot)
        value_grad = skip * out_grad + scaled_grad * spread
        pre_grad = value_grad * (pre_sig * (1.0 + pre * (1.0 - pre_sig)))
        cotb_ref[:, cols] = conv_back(pre_grad, taps, kernel).astype(bf16)
        rows = conv_sums(pre_grad, raw, kernel) + [gain_row, skip_row]
        rows = rows + [jnp.zeros_like(gain_row)] * (tap_sums_ref.shape[0] - len(rows))
        tap_sums_ref[:, cols] = tap_sums_ref[:, cols] + jnp.concatenate(rows, axis=0)

    lower = iota((length, length), 0) >= iota((length, length), 1)
    score_low = jnp.where(lower, score_ref[...], 0.0).astype(bf16)
    shared_grad = jnp.concatenate(
        [dot(score_low, part.out_map, (0, 0)), dot(score_low, part.in_map)], axis=1
    )
    if joined:
        shared_grad = shared_grad + joined_ref[...]
    if primary:
        bc_pre, bc_sig = part.bc_pre, part.bc_sig
        bc_grad = shared_grad * (bc_sig * (1.0 + bc_pre * (1.0 - bc_sig)))
        cota_ref[:, inner:] = conv_back(bc_grad, cbc_ref, kernel).astype(bf16)
        rows = conv_sums(bc_grad, part.bc_rows, kernel)
        rows = rows + [jnp.zeros_like(rows[0])] * (bc_out_ref.shape[0] - len(rows))
        bc_out_ref[...] = bc_out_ref[...] + jnp.concatenate(rows, axis=0)
    else:
        bc_out_ref[...] = shared_grad
    decay_grad = dot_exact(lower.astype(f32), cum_grad, (0, 0))
    raw_grad = (step_grad + decay_grad * part.rate) * sigmoid(part.step_raw)
    cotb_ref[:, inner:] = raw_grad.astype(bf16)
    rows = [
        part.rate * jnp.sum(step * decay_grad, axis=0, keepdims=True),
        jnp.sum(raw_grad, axis=0, keepdims=True),
    ]
    rows = rows + [jnp.zeros_like(rows[0])] * (tap_sums_ref.shape[0] - len(rows))
    tap_sums_ref[:, inner:] = tap_sums_ref[:, inner:] + jnp.concatenate(rows, axis=0)


def product_kernel(*refs, order, scaled, inner_all):
    if scaled:
        place_ref, turned_ref, mine_ref, peer_ref, grad_ref, more_ref = refs[:6]
        keep_ref, send_ref, sum_ref, scaled_ref = refs[6:]

        @pl.when(pl.program_id(0) == 0)
        def scale():
            half = turned_ref.shape[1] // 2
            for slot in range(2):
                mine = mine_ref[slot * sub : slot * sub + 1, :]
                peer = peer_ref[(1 - slot) * sub : (1 - slot) * sub + 1, :]
                row = lax.rsqrt((mine + peer) / inner_all + norm_eps)
                cols = slice(slot * half, (slot + 1) * half)
                scaled_ref[:, cols] = (turned_ref[:, cols].astype(f32) * row).astype(bf16)

        half = turned_ref.shape[1] // 2
        product = dot(scaled_ref[:, :half], grad_ref[...]) + dot(
            scaled_ref[:, half:], more_ref[...]
        )
    else:
        place_ref, turned_ref, grad_ref, keep_ref, send_ref, sum_ref = refs
        product = dot(turned_ref[...], grad_ref[...])
    place = place_ref[0]
    rows = keep_ref.shape[1]
    sum_ref[...] = product.astype(bf16)
    for at, mask in enumerate(order):
        start = pl.multiple_of((place ^ mask) * rows, 32)
        keep_ref[at] = sum_ref[pl.ds(start, rows), :]
        start = pl.multiple_of((place ^ mask ^ 1) * rows, 32)
        send_ref[at] = sum_ref[pl.ds(start, rows), :]


def whole(array):
    return pl.BlockSpec(array.shape, lambda step, *_: (0,) * array.ndim, pipeline_mode=pl.Buffered(1))


def rows_spec(length, width, column=0):
    return pl.BlockSpec((length, width), lambda step, *_: (step, column))


def fixed_spec(shape):
    return pl.BlockSpec(shape, lambda step, *_: (0,) * len(shape))


def any_spec():
    return pl.BlockSpec(memory_space=pl.ANY)


def stat_spec(length, slots, back):
    return pl.BlockSpec((sub, length), lambda step, *_: (lax.rem(step + slots - back, slots), 0))


def call_params(kinds=("arbitrary",)):
    return pltpu.CompilerParams(dimension_semantics=kinds, vmem_limit_bytes=56 * 1024 * 1024)


def run_forward(place, normed, weights, bc_from, tables, seq_len, state, kernel):
    table, _ = tables
    inner = table.shape[1] - lanes
    split = isinstance(weights[0], (list, tuple))
    primary = bc_from is None
    depth = normed[0].shape[1]
    rows = sum(part.shape[0] for part in normed)
    if split:
        widths = [group[0].shape[1] for group in weights]
        prefix, ins = [place], [*normed, *weights[0], *weights[1]]
        specs = [whole(part) for part in normed] + [any_spec()] * 16
    else:
        widths = [array.shape[1] for array in weights]
        prefix, ins = [], [*normed, *weights]
        specs = [rows_spec(seq_len, depth)] + [whole(array) for array in weights]
    if not primary:
        ins.append(bc_from)
        specs.append(rows_spec(seq_len, 2 * state, inner // (2 * state)))
    for array in tables:
        ins.append(array)
        specs.append(whole(array))
    outs = [(widths[0], f32), (widths[1], f32), (inner, f32), (inner, f32)]
    out_specs = [rows_spec(seq_len, width) for width, _ in outs]
    out_shape = [jax.ShapeDtypeStruct((rows, width), kind) for width, kind in outs]
    scratch = []
    if split:
        out_specs = out_specs + [fixed_spec((depth, width)) for width in widths]
        out_shape = out_shape + [jax.ShapeDtypeStruct((depth, width), bf16) for width in widths]
        scratch = [pltpu.SemaphoreType.DMA((2, 8))]
        if primary:
            out_specs.append(pl.BlockSpec((depth, seq_len), lambda step, *_: (0, step)))
            out_shape.append(jax.ShapeDtypeStruct((depth, rows), bf16))
    return pl.pallas_call(
        functools.partial(
            forward_kernel, inner=inner, state=state, kernel=kernel, split=split, primary=primary
        ),
        grid_spec=pltpu.PrefetchScalarGridSpec(
            num_scalar_prefetch=len(prefix),
            grid=(rows // seq_len,),
            in_specs=specs,
            out_specs=out_specs,
            scratch_shapes=scratch,
        ),
        out_shape=out_shape,
        compiler_params=call_params(),
        name="kf1" if primary else "kf2",
    )(*prefix, *ins)


def run_gate(place, cot, weights, gated, taps, seq_len, kernel):
    rows, inner = gated[0].shape
    slots, width = rows // seq_len, cot[0].shape[1]
    blocks = len(gated)
    split = isinstance(weights[0], (list, tuple))
    prefix, ins, scratch = [], [*cot], []
    if split:
        prefix = [place]
        specs = [whole(part) for part in cot]
        for group in weights:
            ins.extend(group)
            specs.extend([any_spec()] * 8)
        scratch = [pltpu.SemaphoreType.DMA((blocks, 8))]
    else:
        ins.extend(weights)
        specs = [rows_spec(seq_len, width)] + [whole(array) for array in weights]
    ins.extend(gated)
    specs.extend([rows_spec(seq_len, inner)] * blocks)
    ins.extend(taps)
    specs.extend([whole(table) for table in taps])
    return pl.pallas_call(
        functools.partial(gate_kernel, kernel=kernel, split=split, blocks=blocks),
        grid_spec=pltpu.PrefetchScalarGridSpec(
            num_scalar_prefetch=len(prefix),
            grid=(slots,),
            in_specs=specs,
            out_specs=[rows_spec(seq_len, inner)] * blocks
            + [
                rows_spec(sub, seq_len),
                pl.BlockSpec((blocks * inner, seq_len), lambda step, *_: (0, step)),
            ]
            + [rows_spec(seq_len, inner)] * blocks
            + [fixed_spec((inner, width))] * (blocks if split else 0),
            scratch_shapes=scratch,
        ),
        out_shape=[jax.ShapeDtypeStruct((rows, inner), f32)] * blocks
        + [
            jax.ShapeDtypeStruct((slots * sub, seq_len), f32),
            jax.ShapeDtypeStruct((blocks * inner, rows), bf16),
        ]
        + [jax.ShapeDtypeStruct((rows, inner), bf16)] * blocks
        + [jax.ShapeDtypeStruct((inner, width), bf16)] * (blocks if split else 0),
        compiler_params=call_params(),
        name="kgt",
    )(*prefix, *ins)


def run_backward(stats, turned, proj, bc_from, joined, plain, grad, tables, seq_len, state, kernel, inner_all):
    taps, cbc = tables
    rows, inner = plain.shape
    slots = rows // seq_len
    primary = bc_from is None
    ins = [*stats, *proj]
    specs = [stat_spec(seq_len, slots, back if turned else 0) for back in range(len(stats))]
    specs = specs + [rows_spec(seq_len, array.shape[1]) for array in proj]
    if not primary:
        ins.append(bc_from)
        specs.append(rows_spec(seq_len, 2 * state, inner // (2 * state)))
    if joined is not None:
        ins.append(joined)
        specs.append(rows_spec(seq_len, 2 * state))
    ins.extend([plain, grad])
    specs.extend([rows_spec(seq_len, inner)] * 2)
    for table in tables:
        ins.append(table)
        specs.append(whole(table))
    bc_shape = cbc.shape if primary else (rows, 2 * state)
    return pl.pallas_call(
        functools.partial(
            backward_kernel,
            inner=inner,
            state=state,
            kernel=kernel,
            inner_all=inner_all,
            stat_parts=len(stats),
            primary=primary,
            joined=joined is not None,
        ),
        grid=(slots,),
        in_specs=specs,
        out_specs=[
            rows_spec(seq_len, proj[0].shape[1]),
            rows_spec(seq_len, proj[1].shape[1]),
            fixed_spec(taps.shape),
            fixed_spec(cbc.shape) if primary else rows_spec(seq_len, 2 * state),
        ],
        out_shape=[
            jax.ShapeDtypeStruct((rows, proj[0].shape[1]), bf16),
            jax.ShapeDtypeStruct((rows, proj[1].shape[1]), bf16),
            jax.ShapeDtypeStruct(taps.shape, f32),
            jax.ShapeDtypeStruct(bc_shape, f32),
        ],
        scratch_shapes=[pltpu.VMEM((seq_len, seq_len), f32)],
        compiler_params=call_params(),
        name="kb1" if primary else "kb2",
    )(*ins)


def run_product(place, turned, grads, order, stats=(), part=0, parts=1, inner_all=1):
    tokens = turned.shape[1]
    depth = turned.shape[0] // parts
    cols = grads[0].shape[1]
    tile = 512 if cols % 512 == 0 else cols
    rows = depth // 8
    block = pl.BlockSpec((4, rows, tile), lambda step, *_: (0, 0, step))
    scratch = [pltpu.VMEM((depth, tile), bf16)]
    if stats:
        scratch.append(pltpu.VMEM((depth, tokens), bf16))
    return pl.pallas_call(
        functools.partial(
            product_kernel, order=order, scaled=bool(stats), inner_all=inner_all
        ),
        grid_spec=pltpu.PrefetchScalarGridSpec(
            num_scalar_prefetch=1,
            grid=(cols // tile,),
            in_specs=[
                pl.BlockSpec(
                    (depth, tokens), lambda step, *_: (part, 0), pipeline_mode=pl.Buffered(1)
                )
            ]
            + [whole(array) for array in stats]
            + [pl.BlockSpec((grad.shape[0], tile), lambda step, *_: (0, step)) for grad in grads],
            out_specs=[block, block],
            scratch_shapes=scratch,
        ),
        out_shape=[jax.ShapeDtypeStruct((4, rows, cols), bf16)] * 2,
        compiler_params=call_params(),
    )(place, turned, *stats, *grads)


def adam_parts(parameter, first, root, gradient, learn_rate, decay_coef):
    first_mom = beta_one * first + (1.0 - beta_one) * gradient
    second_mom = beta_two * root * root + (1.0 - beta_two) * gradient * gradient
    second_root = jnp.sqrt(second_mom)
    first_hat = first_mom / (1.0 - beta_one**step_count)
    second_hat = second_mom / (1.0 - beta_two**step_count)
    updated = parameter - learn_rate * (
        first_hat / (jnp.sqrt(second_hat) + adam_eps) + decay_coef * parameter
    )
    return updated, first_mom, second_root


def adam_update(parameter, moments, gradient, learn_rate, decay_coef):
    updated, first_mom, second_root = adam_parts(
        parameter, moments[0], moments[1], gradient, learn_rate, decay_coef
    )
    return (updated, jnp.stack([first_mom, second_root]))


def adam_kernel(*refs, inner, count):
    terms_a, terms_b = refs[:count], refs[count : 2 * count]
    home_a, home_b, zx_ref, zx_mom_ref, dt_ref, dt_mom_ref = refs[2 * count : 2 * count + 6]
    zx_out, zx_mom_out, dt_out, dt_mom_out = refs[2 * count + 6 :]

    def total(terms, home, start, stop):
        value = home[:, start:stop].astype(f32)
        for term in terms:
            value = value + term[..., start:stop].reshape(value.shape).astype(f32)
        return value

    for plane, (terms, home) in enumerate(((terms_a, home_a), (terms_b, home_b))):
        zx_out[:, plane, :], zx_mom_out[0, :, plane, :], zx_mom_out[1, :, plane, :] = adam_parts(
            zx_ref[:, plane, :],
            zx_mom_ref[0, :, plane, :],
            zx_mom_ref[1, :, plane, :],
            total(terms, home, 0, inner),
            rate_matrix,
            weight_decay,
        )
    grad = total(terms_b, home_b, inner, inner + lanes)[:, : dt_ref.shape[1]]
    dt_out[...], dt_mom_out[0], dt_mom_out[1] = adam_parts(
        dt_ref[...], dt_mom_ref[0], dt_mom_ref[1], grad, rate_matrix, weight_decay
    )


def run_adam(terms_a, terms_b, home_a, home_b, arrays, inner):
    rows = home_a.shape[0]
    tile = rows // 4

    def piece(array):
        width = array.shape[-1]
        if array.ndim == 3:
            return pl.BlockSpec((1, tile, width), lambda step: (0, step, 0))
        return pl.BlockSpec((tile, width), lambda step: (step, 0))

    def tiled(array, axis):
        shape = tuple(tile if at == axis else size for at, size in enumerate(array.shape))
        return pl.BlockSpec(
            shape, lambda step: tuple(step if at == axis else 0 for at in range(array.ndim))
        )

    state = [tiled(array, at % 2) for at, array in enumerate(arrays)]
    ins = [*terms_a, *terms_b, home_a, home_b]
    return pl.pallas_call(
        functools.partial(adam_kernel, inner=inner, count=len(terms_a)),
        grid=(4,),
        in_specs=[piece(array) for array in ins] + state,
        out_specs=state,
        out_shape=[jax.ShapeDtypeStruct(array.shape, f32) for array in arrays],
        compiler_params=call_params(),
        name="kad",
    )(*ins, *arrays)


def swap_by(values, axis, count, mask):
    return lax.ppermute(values, axis, [(i, i ^ mask) for i in range(count)])


def after(values, *earlier):
    return lax.optimization_barrier((values, *earlier))[0]


def pad_to(values, rows, cols):
    return jnp.pad(values, ((0, rows - values.shape[0]), (0, cols - values.shape[1])))


def gather_near(piece, way):
    other = 6 - way
    near = swap_by(piece, DP, 8, way)
    side = swap_by(piece, DP, 8, other)
    return near, side


def gather_rest(piece, near, side, way):
    far = swap_by(near, DP, 8, 6 - way)
    mine = [piece, near, side, far] if way == 2 else [piece, side, near, far]
    return mine + [swap_by(values, DP, 8, 1) for values in mine]


def order_of(way):
    return (0, 6 - way, way, 6)


def wide_sum(*parts):
    total = parts[0].astype(f32)
    for part in parts[1:]:
        total = total + part.astype(f32)
    return total


def scatter_first(keep, send):
    got = swap_by(send, DP, 8, 1)
    return wide_sum(keep[2:], got[2:]).astype(bf16), (keep, got)


def scatter_second(away, terms, way):
    terms = (*terms, swap_by(away, DP, 8, way))
    away = wide_sum(*[term[1] for term in terms]).astype(bf16)
    return away, terms


def scatter_last(away, terms, way):
    return (*terms, swap_by(away, DP, 8, 6 - way))


def scatter_third(away, terms, way):
    terms = scatter_last(away, terms, way)
    return wide_sum(*[term[0] for term in terms[:-1]], terms[-1])


def branch_kernel(*refs):
    count = (len(refs) - 2) // 2
    own_ref, peer_ref = refs[-2:]
    total = dot(refs[0][...], refs[count][...])
    for at in range(1, count):
        total = total + dot(refs[at][...], refs[count + at][...])
    half = own_ref.shape[0]
    own_ref[...] = total[:half]
    peer_ref[...] = total[half:].astype(bf16)


def cotangent_kernel(*refs):
    count = (len(refs) - 5) // 2
    mine_ref, other_ref, own_ref, peer_ref, gain_ref = refs[-5:]
    total = dot(refs[0][...], refs[count][...], (1, 1))
    for at in range(1, count):
        total = total + dot(refs[at][...], refs[count + at][...], (1, 1))
    half = own_ref.shape[0]
    own_ref[...] = total[:half]
    peer_ref[...] = total[half:].astype(bf16)
    gain = jnp.sum(
        total[:half] * mine_ref[...].astype(f32) + total[half:] * other_ref[...].astype(f32),
        axis=0,
        keepdims=True,
    )
    gain_ref[...] = jnp.broadcast_to(gain, gain_ref.shape)


def run_sum(kernel, left, right, turned, normed=()):
    rows, width = left[0].shape[0], right[0].shape[0] if turned else right[0].shape[1]
    tile = 512
    half = rows // 2
    columns = pl.BlockSpec((half, tile), lambda step: (0, step))
    specs = [whole(array) for array in left]
    for array in right:
        if turned:
            specs.append(pl.BlockSpec((tile, array.shape[1]), lambda step: (step, 0)))
        else:
            specs.append(pl.BlockSpec((array.shape[0], tile), lambda step: (0, step)))
    shapes = [jax.ShapeDtypeStruct((half, width), f32), jax.ShapeDtypeStruct((half, width), bf16)]
    outs = [columns, columns]
    if normed:
        specs = specs + [columns, columns]
        shapes.append(jax.ShapeDtypeStruct((sub, width), f32))
        outs.append(pl.BlockSpec((sub, tile), lambda step: (0, step)))
    return pl.pallas_call(
        kernel,
        grid=(width // tile,),
        in_specs=specs,
        out_specs=outs,
        out_shape=shapes,
        compiler_params=call_params(),
    )(*left, *right, *normed)


def sum_over(values, axis, count):
    if count & (count - 1):
        return lax.psum(values, axis)
    mask = 1
    while mask < count:
        values = values + swap_by(values, axis, count, mask)
        mask = mask * 2
    return values


def shards(
    block_input,
    seq_lengths,
    cotangent,
    norm_gain,
    proj_zx,
    proj_dt,
    proj_bc,
    chan_params,
    conv_bc,
    head_params,
    out_proj,
    gain_moments,
    zx_moments,
    dt_moments,
    bc_moments,
    chan_moments,
    convbc_moments,
    head_moments,
    out_moments,
):
    heads_axis = lax.axis_size(HEAD)
    dp_axis = lax.axis_size(DP)
    slot_count = seq_lengths.shape[0]
    rows_own, model_width = block_input.shape
    rows_dev = rows_own * heads_axis
    seq_len = rows_dev // slot_count
    rows_dp = proj_zx.shape[0]
    inner = chan_params.shape[1]
    inner_all = inner * heads_axis
    heads_loc = head_params.shape[1]
    headdim = inner // heads_loc
    kernel = chan_params.shape[0] - 2
    state = conv_bc.shape[1] // 2
    spot = lax.axis_index(HEAD)
    place = lax.axis_index(DP).astype(jnp.int32).reshape(1)
    paired = heads_axis == 4 and dp_axis == 8 and rows_own == seq_len

    zx_low = proj_zx.astype(bf16)
    piece_a = jnp.concatenate([zx_low[:, 0], proj_bc.astype(bf16)], axis=1)
    piece_b = jnp.concatenate([zx_low[:, 1], pad_to(proj_dt.astype(bf16), rows_dp, lanes)], axis=1)
    out_low = out_proj.astype(bf16)
    taps = pad_to(
        jnp.concatenate([chan_params, jnp.repeat(head_params[2:3], headdim, axis=1)], axis=0),
        sub,
        inner,
    )
    cbc = pad_to(conv_bc, sub, 2 * state)
    table = jnp.concatenate([taps, pad_to(head_params, sub, lanes)], axis=1)

    positions = iota((slot_count, seq_len), 1)
    live_mask = (positions < seq_lengths[:, None]).astype(f32).reshape(rows_dev, 1)
    live_own = lax.dynamic_slice_in_dim(live_mask, spot * rows_own, rows_own, 0)
    gain_float = lax.optimization_barrier(norm_gain.astype(bf16)).astype(f32)
    input_float = block_input.astype(f32)
    inv_own = lax.rsqrt(jnp.mean(input_float * input_float, axis=-1, keepdims=True) + norm_eps)
    own_hat = input_float * inv_own
    normed_own = (own_hat * gain_float[None, :]).astype(bf16)
    cot_float = cotangent.astype(f32)
    cot_own = (cot_float * live_own).astype(bf16)
    tables = (table, cbc)

    if paired:
        more_a = swap_by(zx_low[:, 0], HEAD, 4, 2)
        more_b = swap_by(piece_b, HEAD, 4, 2)
        near_a = gather_near(piece_a, 2)
        near_b = gather_near(piece_b, 4)
        normed_all = (normed_own, swap_by(normed_own, HEAD, 4, 1))
        out_more_low = swap_by(out_low, HEAD, 4, 2)
        tables_more = (swap_by(table, HEAD, 4, 2), cbc)
        own_pieces = (gather_rest(piece_a, *near_a, 2), gather_rest(piece_b, *near_b, 4))
        more_a, more_b = after((more_a, more_b), *near_a, *near_b)
        near_a = gather_near(more_a, 2)
        near_b = gather_near(more_b, 4)
        more_pieces = (gather_rest(more_a, *near_a, 2), gather_rest(more_b, *near_b, 4))
        out_low, out_more_low = after((out_low, out_more_low), *near_a, *near_b)
        near_a = gather_near(out_low, 2)
        near_b = gather_near(out_more_low, 4)
        out_pieces = (gather_rest(out_low, *near_a, 2), gather_rest(out_more_low, *near_b, 4))
        cot_all = (cot_own, swap_by(cot_own, HEAD, 4, 1))
        proj_a, proj_b, plain, gated, own_a, own_b, turned = run_forward(
            place, normed_all, own_pieces, None, tables, seq_len, state, kernel
        )
        more_proj_a, more_proj_b, more_plain, more_gated, more_a, more_b = run_forward(
            place, normed_all, more_pieces, proj_a, tables_more, seq_len, state, kernel
        )
        grad, more_grad, stats, lifted_turned, lifted, more_lifted, out_a, out_b = run_gate(
            place, cot_all, out_pieces, (gated, more_gated), (table, tables_more[0]), seq_len, kernel
        )
        stat_parts = [stats, swap_by(stats, HEAD, 4, 1)]
        out_own = run_product(
            place, lifted_turned, cot_all, order_of(2), stat_parts, 0, 2, inner_all
        )
        out_more = run_product(
            place, lifted_turned, cot_all, order_of(4), stat_parts, 1, 2, inner_all
        )
        lifted, more_lifted = after((lifted, more_lifted), out_own[0], out_more[0])
        branch_own, branch_peer = run_sum(
            branch_kernel, (lifted, more_lifted), (out_a, out_b), False
        )
        branch_own = branch_own + swap_by(branch_peer, HEAD, 4, 1).astype(f32)
        square_own = stats[:1] + stat_parts[1][sub : sub + 1]
        gate_own = lax.rsqrt(square_own / inner_all + norm_eps).reshape(seq_len, 1)
        out_own = scatter_first(*out_own)
        out_more = scatter_first(*out_more)
        more_grad = after(more_grad, branch_peer, out_own[0], out_more[0])
        more_cot_a, more_cot_b, more_sums, bc_part = run_backward(
            stat_parts,
            True,
            (more_proj_a, more_proj_b),
            proj_a,
            None,
            more_plain,
            more_grad,
            tables_more,
            seq_len,
            state,
            kernel,
            inner_all,
        )
        grad_more_a = run_product(place, turned, (more_cot_a,), order_of(2))
        grad_more_b = run_product(place, turned, (more_cot_b,), order_of(4))
        out_own = scatter_second(*out_own, 2)
        out_more = scatter_second(*out_more, 4)
        grad = after(grad, grad_more_a[0], grad_more_b[0], out_own[0], out_more[0])
        cot_a, cot_b, own_sums, cbc_sums = run_backward(
            stat_parts,
            True,
            (proj_a, proj_b),
            None,
            bc_part,
            plain,
            grad,
            tables,
            seq_len,
            state,
            kernel,
            inner_all,
        )
        grad_more_a = scatter_first(*grad_more_a)
        grad_more_b = scatter_first(*grad_more_b)
        out_away = scatter_third(*out_more, 4).astype(bf16)
        cot_a, cot_b = after((cot_a, cot_b), out_away, grad_more_a[0], grad_more_b[0])
        grad_own_a = run_product(place, turned, (cot_a,), order_of(2))
        grad_own_b = run_product(place, turned, (cot_b,), order_of(4))
        grad_more_a = scatter_second(*grad_more_a, 2)
        grad_more_b = scatter_second(*grad_more_b, 4)
        grad_own_a = scatter_first(*grad_own_a)
        grad_own_b = scatter_first(*grad_own_b)
        cot_a, cot_b, more_cot_a, more_cot_b = after(
            (cot_a, cot_b, more_cot_a, more_cot_b),
            grad_more_a[0],
            grad_more_b[0],
            grad_own_a[0],
            grad_own_b[0],
        )
        grad_out = scatter_third(*out_own, 2) + swap_by(out_away, HEAD, 4, 2).astype(f32)
        cot_whole, cot_peer, grad_gain = run_sum(
            cotangent_kernel,
            (more_cot_a, more_cot_b, cot_a, cot_b),
            (more_a, more_b, own_a, own_b),
            True,
            normed_all,
        )
        cot_whole = cot_whole + swap_by(cot_peer, HEAD, 4, 1).astype(f32)
        away_a = scatter_third(*grad_more_a, 2).astype(bf16)
        away_b = scatter_third(*grad_more_b, 4).astype(bf16)
        home_a = swap_by(away_a, HEAD, 4, 2)
        home_b = swap_by(away_b, HEAD, 4, 2)
        grad_own_a = scatter_second(*grad_own_a, 2)
        grad_own_b = scatter_second(*grad_own_b, 4)
        terms_a = scatter_last(*grad_own_a, 2)
        terms_b = scatter_last(*grad_own_b, 4)
        zx_next, zx_state, dt_next, dt_state = run_adam(
            terms_a, terms_b, home_a, home_b, (proj_zx, zx_moments, proj_dt, dt_moments), inner
        )
        grad_bc = wide_sum(*[term[0, :, inner:] for term in terms_a[:-1]], terms_a[-1][:, inner:])
        bc_low = grad_bc.astype(bf16)
        for mask in (1, 2, 3):
            grad_bc = grad_bc + swap_by(bc_low, HEAD, 4, mask).astype(f32)
        wide = inner + lanes
        small = jnp.concatenate([more_sums, own_sums, cbc_sums, grad_gain], axis=1)
        small = small + swap_by(small, DP, 8, 1)
        small = small + sum(swap_by(small, DP, 8, mask) for mask in (2, 4, 6))
        both = small[:, 2 * wide :]
        both = both + sum(swap_by(both, HEAD, 4, mask) for mask in (1, 2, 3))
        own_sums = small[:, wide : 2 * wide] + swap_by(small[:, :wide], HEAD, 4, 2)
        cbc_sums, grad_gain = both[:, : 2 * state], both[0, 2 * state :]
    else:
        normed_all = lax.all_gather(normed_own, HEAD, axis=0, tiled=True)
        cot_all = lax.all_gather(cot_own, HEAD, axis=0, tiled=True)
        own_a = lax.all_gather(piece_a, DP, axis=0, tiled=True)
        own_b = lax.all_gather(piece_b, DP, axis=0, tiled=True)
        out_full = lax.all_gather(out_low, DP, axis=0, tiled=True)
        proj_a, proj_b, plain, gated = run_forward(
            None, (normed_all,), (own_a, own_b), None, tables, seq_len, state, kernel
        )
        grad, stats, _, lifted = run_gate(
            None, (cot_all,), (out_full,), (gated,), (table,), seq_len, kernel
        )
        branch = dot(lifted, out_full)
        stats = lax.psum(stats, HEAD)
        square = stats.reshape(slot_count, sub, seq_len)[:, 0].reshape(rows_dev, 1)
        gate_all = lax.rsqrt(square / inner_all + norm_eps)
        gate_own = lax.dynamic_slice_in_dim(gate_all, spot * rows_own, rows_own, 0)
        cot_gate = (cot_all.astype(f32) * gate_all).astype(bf16)
        cot_a, cot_b, own_sums, cbc_sums = run_backward(
            [stats],
            False,
            (proj_a, proj_b),
            None,
            None,
            plain,
            grad,
            tables,
            seq_len,
            state,
            kernel,
            inner_all,
        )
        cot_input = dot(cot_a, own_a, (1, 1)) + dot(cot_b, own_b, (1, 1))
        grad_gain = jnp.sum(cot_input * normed_all.astype(f32), axis=0)

        def scatter(values, axis):
            return lax.psum_scatter(
                values.astype(bf16), axis, scatter_dimension=0, tiled=True
            ).astype(f32)

        cot_whole = scatter(cot_input, HEAD)
        branch_own = scatter(branch, HEAD)
        grad_out = scatter(dot(lifted, cot_gate, (0, 0)), DP)
        sum_a = scatter(dot(normed_all, cot_a, (0, 0)), DP)
        sum_b = scatter(dot(normed_all, cot_b, (0, 0)), DP)
        grad_zx = jnp.stack([sum_a[:, :inner], sum_b[:, :inner]], axis=1)
        grad_dt = sum_b[:, inner:][:, :heads_loc]
        zx_next, zx_state = adam_update(proj_zx, zx_moments, grad_zx, rate_matrix, weight_decay)
        dt_next, dt_state = adam_update(proj_dt, dt_moments, grad_dt, rate_matrix, weight_decay)
        grad_bc = lax.psum(sum_a[:, inner:].astype(bf16), HEAD).astype(f32)
        own_sums = sum_over(own_sums, DP, dp_axis)
        cbc_sums = sum_over(sum_over(cbc_sums, DP, dp_axis), HEAD, heads_axis)
        grad_gain = sum_over(sum_over(grad_gain, DP, dp_axis), HEAD, heads_axis)

    block_output = (input_float + live_own * (branch_own * gate_own)).astype(bf16)
    lift_own = cot_whole * gain_float[None, :]
    row_dot = jnp.sum(lift_own * own_hat, axis=-1, keepdims=True)
    input_grad = cot_float + inv_own * (lift_own - own_hat * row_dot / model_width)

    grad_convbc = cbc_sums[: kernel + 1]
    grad_gain = grad_gain / gain_float
    grad_chan = own_sums[: kernel + 2, :inner]
    grad_skip = jnp.sum(own_sums[kernel + 2, :inner].reshape(heads_loc, headdim), axis=1)
    grad_head = jnp.concatenate(
        [own_sums[:2, inner : inner + heads_loc], grad_skip[None, :]], axis=0
    )

    gain_next, gain_state = adam_update(norm_gain, gain_moments, grad_gain, rate_vector, 0.0)
    bc_next, bc_state = adam_update(proj_bc, bc_moments, grad_bc, rate_matrix, weight_decay)
    chan_next, chan_state = adam_update(chan_params, chan_moments, grad_chan, rate_vector, 0.0)
    convbc_next, convbc_state = adam_update(conv_bc, convbc_moments, grad_convbc, rate_vector, 0.0)
    head_next, head_state = adam_update(head_params, head_moments, grad_head, rate_vector, 0.0)
    outproj_next, outproj_state = adam_update(
        out_proj, out_moments, grad_out, rate_matrix, weight_decay
    )
    return (
        block_output,
        input_grad,
        gain_next,
        gain_state,
        zx_next,
        zx_state,
        dt_next,
        dt_state,
        bc_next,
        bc_state,
        chan_next,
        chan_state,
        convbc_next,
        convbc_state,
        head_next,
        head_state,
        outproj_next,
        outproj_state,
    )


def solution(mesh):
    placed = (
        P((DP, HEAD), None),
        P(DP),
        P((DP, HEAD), None),
        P(),
        P(DP, None, HEAD),
        P(DP, HEAD),
        P(DP, None),
        P(None, HEAD),
        P(),
        P(None, HEAD),
        P((HEAD, DP), None),
        P(),
        P(None, DP, None, HEAD),
        P(None, DP, HEAD),
        P(None, DP, None),
        P(None, None, HEAD),
        P(),
        P(None, None, HEAD),
        P(None, (HEAD, DP), None),
    )
    return jax.shard_map(
        shards,
        mesh=mesh,
        in_specs=placed,
        out_specs=(
            P((DP, HEAD), None),
            P((DP, HEAD), None),
            P(),
            P(),
            P(DP, None, HEAD),
            P(None, DP, None, HEAD),
            P(DP, HEAD),
            P(None, DP, HEAD),
            P(DP, None),
            P(None, DP, None),
            P(None, HEAD),
            P(None, None, HEAD),
            P(),
            P(),
            P(None, HEAD),
            P(None, None, HEAD),
            P((HEAD, DP), None),
            P(None, (HEAD, DP), None),
        ),
        check_vma=False,
    )
```

```python
import functools
from types import SimpleNamespace

import jax
import jax.numpy as jnp
from jax import lax
from jax.experimental import pallas as pl
from jax.experimental.pallas import tpu as pltpu
from jax.sharding import PartitionSpec as P


norm_eps = 1e-05
beta_one = 0.9
beta_two = 0.95
adam_eps = 1e-08
step_count = 3.0
rate_matrix = 0.005
rate_vector = 0.2
weight_decay = 0.1
lanes = 128
HEAD = "head"
DP = "dp"
WEIGHT_PLACE, TOKEN_PLACE = 2, 1
sub = 8
f32 = jnp.float32
bf16 = jnp.bfloat16


def dot(lhs, rhs, over=(1, 0)):
    return lax.dot_general(
        lhs, rhs, (((over[0],), (over[1],)), ((), ())), preferred_element_type=f32
    )


def dot_exact(lhs, rhs, over=(1, 0)):
    return lax.dot_general(
        lhs,
        rhs,
        (((over[0],), (over[1],)), ((), ())),
        precision=lax.Precision.HIGHEST,
        preferred_element_type=f32,
    )


def dot_chosen(lhs, chosen):
    high = lhs.astype(bf16)
    rest = lhs - high.astype(f32)
    middle = rest.astype(bf16)
    low = (rest - middle.astype(f32)).astype(bf16)
    return dot(high, chosen) + dot(middle, chosen) + dot(low, chosen)


def iota(shape, axis):
    return lax.broadcasted_iota(jnp.int32, shape, axis)


def later(values, count):
    if count == 0:
        return values
    rolled = pltpu.roll(values, count, 0)
    return jnp.where(iota(values.shape, 0) >= count, rolled, 0.0)


def earlier(values, count):
    if count == 0:
        return values
    length = values.shape[0]
    rolled = pltpu.roll(values, length - count, 0)
    return jnp.where(iota(values.shape, 0) < length - count, rolled, 0.0)


def conv(values, taps, kernel):
    summed = taps[kernel : kernel + 1] + taps[kernel - 1 : kernel] * values
    for offset in range(kernel - 1):
        summed = summed + taps[offset : offset + 1] * later(values, kernel - 1 - offset)
    return summed


def conv_back(grads, taps, kernel):
    summed = taps[kernel - 1 : kernel] * grads
    for offset in range(kernel - 1):
        summed = summed + taps[offset : offset + 1] * earlier(grads, kernel - 1 - offset)
    return summed


def conv_sums(grads, values, kernel):
    rows = [
        jnp.sum(grads * later(values, kernel - 1 - offset), axis=0, keepdims=True)
        for offset in range(kernel)
    ]
    rows.append(jnp.sum(grads, axis=0, keepdims=True))
    return rows


def sigmoid(values):
    return 1.0 / (1.0 + jnp.exp(-values))


def shared_parts(bc_rows, step_raw, cbc_ref, head_ref, state, kernel):
    step_raw = step_raw + head_ref[1:2, :]
    length = bc_rows.shape[0]
    bc_pre = conv(bc_rows, cbc_ref, kernel)
    bc_sig = sigmoid(bc_pre)
    shared = bc_pre * bc_sig
    step = jnp.maximum(step_raw, 0.0) + jnp.log1p(jnp.exp(-jnp.abs(step_raw)))
    rate = -jnp.exp(head_ref[0:1, :])
    lower = (iota((length, length), 0) >= iota((length, length), 1)).astype(f32)
    cum = dot_exact(lower, step * rate)
    in_map = shared[:, :state].astype(bf16)
    out_map = shared[:, state:].astype(bf16)
    scores = dot(out_map, in_map, (1, 1)) * lower
    return SimpleNamespace(
        bc_rows=bc_rows,
        bc_pre=bc_pre,
        bc_sig=bc_sig,
        step_raw=step_raw,
        step=step,
        rate=rate,
        cum=cum,
        cum_t=cum.T,
        in_map=in_map,
        out_map=out_map,
        scores=scores,
    )


def pick(values, pair, first):
    return jnp.where(
        first, values[:, 2 * pair : 2 * pair + 1], values[:, 2 * pair + 1 : 2 * pair + 2]
    )


def blocks_of(length):
    half = length // 2
    return [((0, half), (0, half)), ((half, length), (0, length))]


def place_pieces(place, pieces, target, sems):
    copies = []
    for at, (mask, ref) in enumerate(pieces):
        rows = ref.shape[0]
        start = pl.multiple_of((place ^ mask) * rows, 32)
        copies.append(
            pltpu.make_async_copy(ref, target.at[pl.ds(start, rows), :], sems.at[at])
        )
    for copy in copies:
        copy.start()
    return copies


piece_masks = (0, 2, 4, 6, 1, 3, 5, 7)


def forward_kernel(*refs, inner, state, kernel, split, primary):
    if split:
        place_ref, x_ref, peer_ref = refs[:3]
        pieces_a, pieces_b = refs[3:11], refs[11:19]
        rest = refs[19:]
    else:
        x_ref, wa_ref, wb_ref = refs[:3]
        rest = refs[3:]
    if not primary:
        bc_ref = rest[0]
        rest = rest[1:]
    taps_ref, cbc_ref, proja_ref, projb_ref, y_ref, gated_ref = rest[:6]
    head_ref = taps_ref.at[:, pl.ds(inner, lanes)]
    if split:
        wa_ref, wb_ref = rest[6:8]
        sems = rest[-1]

        @pl.when(pl.program_id(0) == 0)
        def assemble():
            place = place_ref[0]
            copies = place_pieces(place, list(zip(piece_masks, pieces_a)), wa_ref, sems.at[0])
            copies = copies + place_pieces(
                place, list(zip(piece_masks, pieces_b)), wb_ref, sems.at[1]
            )
            for copy in copies:
                copy.wait()

    length = x_ref.shape[0]
    rows = x_ref[...]
    if split:
        rows = jnp.where(pl.program_id(0) == 0, rows, peer_ref[...])
        if primary:
            turned_ref = rest[8]
            for start in range(0, rows.shape[1], lanes):
                turned_ref[start : start + lanes, :] = (
                    rows[:, start : start + lanes].astype(f32).T.astype(bf16)
                )
    for weights, target in ((wa_ref, proja_ref), (wb_ref, projb_ref)):
        width = weights.shape[1]
        for start in range(0, width, 256):
            stop = min(width, start + 256)
            target[:, start:stop] = dot(rows, weights[:, start:stop])
    bc_rows = proja_ref[:, inner:] if primary else bc_ref[...]
    part = shared_parts(bc_rows, projb_ref[:, inner:], cbc_ref, head_ref, state, kernel)
    step, cum, cum_t, scores = part.step, part.cum, part.cum_t, part.scores
    first = iota((length, lanes), 1) < lanes // 2
    for pair in range(inner // lanes):
        cols = slice(pair * lanes, (pair + 1) * lanes)
        taps = taps_ref[:, cols]
        gate = proja_ref[:, cols]
        values = conv(projb_ref[:, cols], taps, kernel)
        values = values * sigmoid(values)
        scaled = values * pick(step, pair, first)
        halves = (
            jnp.where(first, scaled, 0.0).astype(bf16),
            jnp.where(first, 0.0, scaled).astype(bf16),
        )
        pieces = []
        for (r0, r1), (c0, c1) in blocks_of(length):
            total = None
            for side in range(2):
                head = 2 * pair + side
                gap = cum[r0:r1, head : head + 1] - cum_t[head : head + 1, c0:c1]
                weights = (scores[r0:r1, c0:c1] * jnp.exp(jnp.minimum(gap, 0.0))).astype(bf16)
                term = dot(weights, halves[side][c0:c1])
                total = term if total is None else total + term
            pieces.append(total)
        output = jnp.concatenate(pieces, axis=0)
        y_ref[:, cols] = output
        gated_ref[:, cols] = (output + taps[kernel + 2 : kernel + 3] * values) * (
            gate * sigmoid(gate)
        )


def gate_kernel(*refs, kernel, split, blocks):
    if split:
        place_ref, cot_ref, peer_ref = refs[:3]
        pieces = [refs[3 + 8 * at : 11 + 8 * at] for at in range(blocks)]
        rest = refs[3 + 8 * blocks :]
    else:
        cot_ref = refs[0]
        out_refs = refs[1 : 1 + blocks]
        rest = refs[1 + blocks :]
    gated_refs, taps_refs = rest[:blocks], rest[blocks : 2 * blocks]
    grad_refs = rest[2 * blocks : 3 * blocks]
    stats_ref, turned_ref = rest[3 * blocks : 3 * blocks + 2]
    rest = rest[3 * blocks + 2 :]
    lifted_refs = rest[:blocks]
    if split:
        out_refs = rest[blocks : 2 * blocks]
        sems = rest[2 * blocks]

        @pl.when(pl.program_id(0) == 0)
        def assemble():
            place = place_ref[0]
            copies = []
            for at in range(blocks):
                copies = copies + place_pieces(
                    place, list(zip(piece_masks, pieces[at])), out_refs[at], sems.at[at]
                )
            for copy in copies:
                copy.wait()

    cot = cot_ref[...]
    if split:
        cot = jnp.where(pl.program_id(0) == 0, cot, peer_ref[...])
    squares, cross = None, None
    for at in range(blocks):
        grad = dot(cot, out_refs[at][...], (1, 1))
        grad_refs[at][...] = grad
        inner = grad.shape[1]
        for start in range(0, inner, lanes):
            cols = slice(start, start + lanes)
            gated = gated_refs[at][:, cols]
            lifted = gated * taps_refs[at][kernel + 1 : kernel + 2, cols]
            lifted_refs[at][:, cols] = lifted.astype(bf16)
            turned_ref[at * inner + start : at * inner + start + lanes, :] = lifted.T.astype(bf16)
            square, product = gated * gated, grad[:, cols] * lifted
            squares = square if squares is None else squares + square
            cross = product if cross is None else cross + product
    ones = jnp.ones((sub, lanes), f32)
    squares = dot_exact(ones, squares, (1, 1))
    cross = dot_exact(ones, cross, (1, 1))
    stats_ref[...] = jnp.where(iota(squares.shape, 0) == 0, squares, cross)


def backward_kernel(*refs, inner, state, kernel, inner_all, stat_parts, primary, joined):
    stat_refs = refs[:stat_parts]
    proja_ref, projb_ref = refs[stat_parts : stat_parts + 2]
    rest = refs[stat_parts + 2 :]
    if not primary:
        bc_ref = rest[0]
        rest = rest[1:]
    if joined:
        joined_ref = rest[0]
        rest = rest[1:]
    y_ref, grad_ref, taps_ref, cbc_ref, cota_ref, cotb_ref, tap_sums_ref = rest[:7]
    bc_out_ref, score_ref = rest[7:9]
    head_ref = taps_ref.at[:, pl.ds(inner, lanes)]
    length = proja_ref.shape[0]
    half_lanes = lanes // 2

    @pl.when(pl.program_id(0) == 0)
    def clear():
        tap_sums_ref[...] = jnp.zeros(tap_sums_ref.shape, f32)
        if primary:
            bc_out_ref[...] = jnp.zeros(bc_out_ref.shape, f32)

    stats = stat_refs[0][...]
    for more in stat_refs[1:]:
        stats = stats + more[...]
    unit = (iota((length, length), 0) == iota((length, length), 1)).astype(f32)
    columns = dot_exact(unit, stats, (1, 1))
    inv = lax.rsqrt(columns[:, 0:1] / inner_all + norm_eps)
    pull = inv * inv * inv * columns[:, 1:2] / inner_all

    bc_rows = proja_ref[:, inner:] if primary else bc_ref[...]
    part = shared_parts(bc_rows, projb_ref[:, inner:], cbc_ref, head_ref, state, kernel)
    step, cum, cum_t, scores = part.step, part.cum, part.cum_t, part.scores
    first = iota((length, lanes), 1) < half_lanes
    score_ref[...] = jnp.zeros(score_ref.shape, f32)
    cum_grad = jnp.zeros((length, lanes), f32)
    step_grad = jnp.zeros((length, lanes), f32)
    for pair in range(inner // lanes):
        cols = slice(pair * lanes, (pair + 1) * lanes)
        taps = taps_ref[:, cols]
        gain = taps[kernel + 1 : kernel + 2]
        skip = taps[kernel + 2 : kernel + 3]
        gate = proja_ref[:, cols]
        raw = projb_ref[:, cols]
        pre = conv(raw, taps, kernel)
        pre_sig = sigmoid(pre)
        values = pre * pre_sig
        spread = pick(step, pair, first)
        scaled = values * spread
        gate_sig = sigmoid(gate)
        lift = gate * gate_sig
        plain = y_ref[:, cols]
        output = plain + skip * values
        gated = output * lift
        normed = gated * inv
        grad = grad_ref[:, cols]
        gain_row = jnp.sum(grad * normed, axis=0, keepdims=True)
        gated_grad = inv * (grad * gain) - gated * pull
        cota_ref[:, cols] = (
            gated_grad * output * (gate_sig * (1.0 + gate * (1.0 - gate_sig)))
        ).astype(bf16)
        out_grad = gated_grad * lift
        skip_row = jnp.sum(out_grad * values, axis=0, keepdims=True)
        out_low = out_grad.astype(bf16)
        scaled_low = scaled.astype(bf16)
        zero = jnp.zeros_like(out_low)
        sides = (jnp.where(first, out_low, zero), jnp.where(first, zero, out_low))
        half = length // 2
        pulled = [jnp.zeros((half, lanes), f32), jnp.zeros((half, lanes), f32)]
        for (r0, r1), (c0, c1) in blocks_of(length):
            score_sum = score_ref[r0:r1, c0:c1]
            for side in range(2):
                head = 2 * pair + side
                gap = cum[r0:r1, head : head + 1] - cum_t[head : head + 1, c0:c1]
                decay = jnp.exp(jnp.minimum(gap, 0.0))
                weights = (scores[r0:r1, c0:c1] * decay).astype(bf16)
                score_sum = score_sum + dot(sides[side][r0:r1], scaled_low[c0:c1], (1, 1)) * decay
                back = dot(weights, sides[side][r0:r1], (0, 0))
                pulled[0] = pulled[0] + back[:half]
                if c1 > half:
                    pulled[1] = pulled[1] + back[half:]
            score_ref[r0:r1, c0:c1] = score_sum
        scaled_grad = jnp.concatenate(pulled, axis=0)
        hot = (
            2 * pair + (iota((lanes, lanes), 0) >= half_lanes).astype(jnp.int32)
            == iota((lanes, lanes), 1)
        ).astype(bf16)
        balance = out_low.astype(f32) * plain - scaled_low.astype(f32) * scaled_grad
        cum_grad = cum_grad + dot_chosen(balance, hot)
        step_grad = step_grad + dot_chosen(values * scaled_grad, hot)
        value_grad = skip * out_grad + scaled_grad * spread
        pre_grad = value_grad * (pre_sig * (1.0 + pre * (1.0 - pre_sig)))
        cotb_ref[:, cols] = conv_back(pre_grad, taps, kernel).astype(bf16)
        rows = conv_sums(pre_grad, raw, kernel) + [gain_row, skip_row]
        rows = rows + [jnp.zeros_like(gain_row)] * (tap_sums_ref.shape[0] - len(rows))
        tap_sums_ref[:, cols] = tap_sums_ref[:, cols] + jnp.concatenate(rows, axis=0)

    lower = iota((length, length), 0) >= iota((length, length), 1)
    score_low = jnp.where(lower, score_ref[...], 0.0).astype(bf16)
    shared_grad = jnp.concatenate(
        [dot(score_low, part.out_map, (0, 0)), dot(score_low, part.in_map)], axis=1
    )
    if joined:
        shared_grad = shared_grad + joined_ref[...]
    if primary:
        bc_pre, bc_sig = part.bc_pre, part.bc_sig
        bc_grad = shared_grad * (bc_sig * (1.0 + bc_pre * (1.0 - bc_sig)))
        cota_ref[:, inner:] = conv_back(bc_grad, cbc_ref, kernel).astype(bf16)
        rows = conv_sums(bc_grad, part.bc_rows, kernel)
        rows = rows + [jnp.zeros_like(rows[0])] * (bc_out_ref.shape[0] - len(rows))
        bc_out_ref[...] = bc_out_ref[...] + jnp.concatenate(rows, axis=0)
    else:
        bc_out_ref[...] = shared_grad
    decay_grad = dot_exact(lower.astype(f32), cum_grad, (0, 0))
    raw_grad = (step_grad + decay_grad * part.rate) * sigmoid(part.step_raw)
    cotb_ref[:, inner:] = raw_grad.astype(bf16)
    rows = [
        part.rate * jnp.sum(step * decay_grad, axis=0, keepdims=True),
        jnp.sum(raw_grad, axis=0, keepdims=True),
    ]
    rows = rows + [jnp.zeros_like(rows[0])] * (tap_sums_ref.shape[0] - len(rows))
    tap_sums_ref[:, inner:] = tap_sums_ref[:, inner:] + jnp.concatenate(rows, axis=0)


def product_kernel(*refs, order, scaled, inner_all):
    if scaled:
        place_ref, turned_ref, mine_ref, peer_ref, grad_ref, more_ref = refs[:6]
        keep_ref, send_ref, sum_ref, scaled_ref = refs[6:]

        @pl.when(pl.program_id(0) == 0)
        def scale():
            half = turned_ref.shape[1] // 2
            for slot in range(2):
                mine = mine_ref[slot * sub : slot * sub + 1, :]
                peer = peer_ref[(1 - slot) * sub : (1 - slot) * sub + 1, :]
                row = lax.rsqrt((mine + peer) / inner_all + norm_eps)
                cols = slice(slot * half, (slot + 1) * half)
                scaled_ref[:, cols] = (turned_ref[:, cols].astype(f32) * row).astype(bf16)

        half = turned_ref.shape[1] // 2
        product = dot(scaled_ref[:, :half], grad_ref[...]) + dot(
            scaled_ref[:, half:], more_ref[...]
        )
    else:
        place_ref, turned_ref, grad_ref, keep_ref, send_ref, sum_ref = refs
        product = dot(turned_ref[...], grad_ref[...])
    place = place_ref[0]
    rows = keep_ref.shape[1]
    sum_ref[...] = product.astype(bf16)
    for at, mask in enumerate(order):
        start = pl.multiple_of((place ^ mask) * rows, 32)
        keep_ref[at] = sum_ref[pl.ds(start, rows), :]
        start = pl.multiple_of((place ^ mask ^ 1) * rows, 32)
        send_ref[at] = sum_ref[pl.ds(start, rows), :]


def whole(array):
    return pl.BlockSpec(array.shape, lambda step, *_: (0,) * array.ndim, pipeline_mode=pl.Buffered(1))


def rows_spec(length, width, column=0):
    return pl.BlockSpec((length, width), lambda step, *_: (step, column))


def fixed_spec(shape):
    return pl.BlockSpec(shape, lambda step, *_: (0,) * len(shape))


def any_spec():
    return pl.BlockSpec(memory_space=pl.ANY)


def stat_spec(length, slots, back):
    return pl.BlockSpec((sub, length), lambda step, *_: (lax.rem(step + slots - back, slots), 0))


def call_params(kinds=("arbitrary",)):
    return pltpu.CompilerParams(dimension_semantics=kinds, vmem_limit_bytes=56 * 1024 * 1024)


def run_forward(place, normed, weights, bc_from, tables, seq_len, state, kernel):
    table, _ = tables
    inner = table.shape[1] - lanes
    split = isinstance(weights[0], (list, tuple))
    primary = bc_from is None
    depth = normed[0].shape[1]
    rows = sum(part.shape[0] for part in normed)
    if split:
        widths = [group[0].shape[1] for group in weights]
        prefix, ins = [place], [*normed, *weights[0], *weights[1]]
        specs = [whole(part) for part in normed] + [any_spec()] * 16
    else:
        widths = [array.shape[1] for array in weights]
        prefix, ins = [], [*normed, *weights]
        specs = [rows_spec(seq_len, depth)] + [whole(array) for array in weights]
    if not primary:
        ins.append(bc_from)
        specs.append(rows_spec(seq_len, 2 * state, inner // (2 * state)))
    for array in tables:
        ins.append(array)
        specs.append(whole(array))
    outs = [(widths[0], f32), (widths[1], f32), (inner, f32), (inner, f32)]
    out_specs = [rows_spec(seq_len, width) for width, _ in outs]
    out_shape = [jax.ShapeDtypeStruct((rows, width), kind) for width, kind in outs]
    scratch = []
    if split:
        out_specs = out_specs + [fixed_spec((depth, width)) for width in widths]
        out_shape = out_shape + [jax.ShapeDtypeStruct((depth, width), bf16) for width in widths]
        scratch = [pltpu.SemaphoreType.DMA((2, 8))]
        if primary:
            out_specs.append(pl.BlockSpec((depth, seq_len), lambda step, *_: (0, step)))
            out_shape.append(jax.ShapeDtypeStruct((depth, rows), bf16))
    return pl.pallas_call(
        functools.partial(
            forward_kernel, inner=inner, state=state, kernel=kernel, split=split, primary=primary
        ),
        grid_spec=pltpu.PrefetchScalarGridSpec(
            num_scalar_prefetch=len(prefix),
            grid=(rows // seq_len,),
            in_specs=specs,
            out_specs=out_specs,
            scratch_shapes=scratch,
        ),
        out_shape=out_shape,
        compiler_params=call_params(),
        name="kf1" if primary else "kf2",
    )(*prefix, *ins)


def run_gate(place, cot, weights, gated, taps, seq_len, kernel):
    rows, inner = gated[0].shape
    slots, width = rows // seq_len, cot[0].shape[1]
    blocks = len(gated)
    split = isinstance(weights[0], (list, tuple))
    prefix, ins, scratch = [], [*cot], []
    if split:
        prefix = [place]
        specs = [whole(part) for part in cot]
        for group in weights:
            ins.extend(group)
            specs.extend([any_spec()] * 8)
        scratch = [pltpu.SemaphoreType.DMA((blocks, 8))]
    else:
        ins.extend(weights)
        specs = [rows_spec(seq_len, width)] + [whole(array) for array in weights]
    ins.extend(gated)
    specs.extend([rows_spec(seq_len, inner)] * blocks)
    ins.extend(taps)
    specs.extend([whole(table) for table in taps])
    return pl.pallas_call(
        functools.partial(gate_kernel, kernel=kernel, split=split, blocks=blocks),
        grid_spec=pltpu.PrefetchScalarGridSpec(
            num_scalar_prefetch=len(prefix),
            grid=(slots,),
            in_specs=specs,
            out_specs=[rows_spec(seq_len, inner)] * blocks
            + [
                rows_spec(sub, seq_len),
                pl.BlockSpec((blocks * inner, seq_len), lambda step, *_: (0, step)),
            ]
            + [rows_spec(seq_len, inner)] * blocks
            + [fixed_spec((inner, width))] * (blocks if split else 0),
            scratch_shapes=scratch,
        ),
        out_shape=[jax.ShapeDtypeStruct((rows, inner), f32)] * blocks
        + [
            jax.ShapeDtypeStruct((slots * sub, seq_len), f32),
            jax.ShapeDtypeStruct((blocks * inner, rows), bf16),
        ]
        + [jax.ShapeDtypeStruct((rows, inner), bf16)] * blocks
        + [jax.ShapeDtypeStruct((inner, width), bf16)] * (blocks if split else 0),
        compiler_params=call_params(),
        name="kgt",
    )(*prefix, *ins)


def run_backward(stats, turned, proj, bc_from, joined, plain, grad, tables, seq_len, state, kernel, inner_all):
    taps, cbc = tables
    rows, inner = plain.shape
    slots = rows // seq_len
    primary = bc_from is None
    ins = [*stats, *proj]
    specs = [stat_spec(seq_len, slots, back if turned else 0) for back in range(len(stats))]
    specs = specs + [rows_spec(seq_len, array.shape[1]) for array in proj]
    if not primary:
        ins.append(bc_from)
        specs.append(rows_spec(seq_len, 2 * state, inner // (2 * state)))
    if joined is not None:
        ins.append(joined)
        specs.append(rows_spec(seq_len, 2 * state))
    ins.extend([plain, grad])
    specs.extend([rows_spec(seq_len, inner)] * 2)
    for table in tables:
        ins.append(table)
        specs.append(whole(table))
    bc_shape = cbc.shape if primary else (rows, 2 * state)
    return pl.pallas_call(
        functools.partial(
            backward_kernel,
            inner=inner,
            state=state,
            kernel=kernel,
            inner_all=inner_all,
            stat_parts=len(stats),
            primary=primary,
            joined=joined is not None,
        ),
        grid=(slots,),
        in_specs=specs,
        out_specs=[
            rows_spec(seq_len, proj[0].shape[1]),
            rows_spec(seq_len, proj[1].shape[1]),
            fixed_spec(taps.shape),
            fixed_spec(cbc.shape) if primary else rows_spec(seq_len, 2 * state),
        ],
        out_shape=[
            jax.ShapeDtypeStruct((rows, proj[0].shape[1]), bf16),
            jax.ShapeDtypeStruct((rows, proj[1].shape[1]), bf16),
            jax.ShapeDtypeStruct(taps.shape, f32),
            jax.ShapeDtypeStruct(bc_shape, f32),
        ],
        scratch_shapes=[pltpu.VMEM((seq_len, seq_len), f32)],
        compiler_params=call_params(),
        name="kb1" if primary else "kb2",
    )(*ins)


def run_product(place, turned, grads, order, stats=(), part=0, parts=1, inner_all=1):
    tokens = turned.shape[1]
    depth = turned.shape[0] // parts
    cols = grads[0].shape[1]
    tile = 512 if cols % 512 == 0 else cols
    rows = depth // 8
    block = pl.BlockSpec((4, rows, tile), lambda step, *_: (0, 0, step))
    scratch = [pltpu.VMEM((depth, tile), bf16)]
    if stats:
        scratch.append(pltpu.VMEM((depth, tokens), bf16))
    return pl.pallas_call(
        functools.partial(
            product_kernel, order=order, scaled=bool(stats), inner_all=inner_all
        ),
        grid_spec=pltpu.PrefetchScalarGridSpec(
            num_scalar_prefetch=1,
            grid=(cols // tile,),
            in_specs=[
                pl.BlockSpec(
                    (depth, tokens), lambda step, *_: (part, 0), pipeline_mode=pl.Buffered(1)
                )
            ]
            + [whole(array) for array in stats]
            + [pl.BlockSpec((grad.shape[0], tile), lambda step, *_: (0, step)) for grad in grads],
            out_specs=[block, block],
            scratch_shapes=scratch,
        ),
        out_shape=[jax.ShapeDtypeStruct((4, rows, cols), bf16)] * 2,
        compiler_params=call_params(),
    )(place, turned, *stats, *grads)


def adam_parts(parameter, first, root, gradient, learn_rate, decay_coef):
    first_mom = beta_one * first + (1.0 - beta_one) * gradient
    second_mom = beta_two * root * root + (1.0 - beta_two) * gradient * gradient
    second_root = jnp.sqrt(second_mom)
    first_hat = first_mom / (1.0 - beta_one**step_count)
    second_hat = second_mom / (1.0 - beta_two**step_count)
    updated = parameter - learn_rate * (
        first_hat / (jnp.sqrt(second_hat) + adam_eps) + decay_coef * parameter
    )
    return updated, first_mom, second_root


def adam_update(parameter, moments, gradient, learn_rate, decay_coef):
    updated, first_mom, second_root = adam_parts(
        parameter, moments[0], moments[1], gradient, learn_rate, decay_coef
    )
    return (updated, jnp.stack([first_mom, second_root]))


def adam_kernel(*refs, inner, count):
    terms_a, terms_b = refs[:count], refs[count : 2 * count]
    home_a, home_b, zx_ref, zx_mom_ref, dt_ref, dt_mom_ref = refs[2 * count : 2 * count + 6]
    zx_out, zx_mom_out, dt_out, dt_mom_out = refs[2 * count + 6 :]

    def total(terms, home, start, stop):
        value = home[:, start:stop].astype(f32)
        for term in terms:
            value = value + term[..., start:stop].reshape(value.shape).astype(f32)
        return value

    for plane, (terms, home) in enumerate(((terms_a, home_a), (terms_b, home_b))):
        zx_out[:, plane, :], zx_mom_out[0, :, plane, :], zx_mom_out[1, :, plane, :] = adam_parts(
            zx_ref[:, plane, :],
            zx_mom_ref[0, :, plane, :],
            zx_mom_ref[1, :, plane, :],
            total(terms, home, 0, inner),
            rate_matrix,
            weight_decay,
        )
    grad = total(terms_b, home_b, inner, inner + lanes)[:, : dt_ref.shape[1]]
    dt_out[...], dt_mom_out[0], dt_mom_out[1] = adam_parts(
        dt_ref[...], dt_mom_ref[0], dt_mom_ref[1], grad, rate_matrix, weight_decay
    )


def run_adam(terms_a, terms_b, home_a, home_b, arrays, inner):
    rows = home_a.shape[0]
    tile = rows // 4

    def piece(array):
        width = array.shape[-1]
        if array.ndim == 3:
            return pl.BlockSpec((1, tile, width), lambda step: (0, step, 0))
        return pl.BlockSpec((tile, width), lambda step: (step, 0))

    def tiled(array, axis):
        shape = tuple(tile if at == axis else size for at, size in enumerate(array.shape))
        return pl.BlockSpec(
            shape, lambda step: tuple(step if at == axis else 0 for at in range(array.ndim))
        )

    state = [tiled(array, at % 2) for at, array in enumerate(arrays)]
    ins = [*terms_a, *terms_b, home_a, home_b]
    return pl.pallas_call(
        functools.partial(adam_kernel, inner=inner, count=len(terms_a)),
        grid=(4,),
        in_specs=[piece(array) for array in ins] + state,
        out_specs=state,
        out_shape=[jax.ShapeDtypeStruct(array.shape, f32) for array in arrays],
        compiler_params=call_params(),
        name="kad",
    )(*ins, *arrays)


def swap_by(values, axis, count, mask):
    return lax.ppermute(values, axis, [(i, i ^ mask) for i in range(count)])


def after(values, *earlier):
    return lax.optimization_barrier((values, *earlier))[0]


def pad_to(values, rows, cols):
    return jnp.pad(values, ((0, rows - values.shape[0]), (0, cols - values.shape[1])))


def gather_near(piece, way):
    other = 6 - way
    near = swap_by(piece, DP, 8, way)
    side = swap_by(piece, DP, 8, other)
    return near, side


def gather_rest(piece, near, side, way):
    far = swap_by(near, DP, 8, 6 - way)
    mine = [piece, near, side, far] if way == 2 else [piece, side, near, far]
    return mine + [swap_by(values, DP, 8, 1) for values in mine]


def order_of(way):
    return (0, 6 - way, way, 6)


def wide_sum(*parts):
    total = parts[0].astype(f32)
    for part in parts[1:]:
        total = total + part.astype(f32)
    return total


def scatter_first(keep, send):
    got = swap_by(send, DP, 8, 1)
    return wide_sum(keep[2:], got[2:]).astype(bf16), (keep, got)


def scatter_second(away, terms, way):
    terms = (*terms, swap_by(away, DP, 8, way))
    away = wide_sum(*[term[1] for term in terms]).astype(bf16)
    return away, terms


def scatter_last(away, terms, way):
    return (*terms, swap_by(away, DP, 8, 6 - way))


def scatter_third(away, terms, way):
    terms = scatter_last(away, terms, way)
    return wide_sum(*[term[0] for term in terms[:-1]], terms[-1])


def branch_kernel(*refs):
    count = (len(refs) - 2) // 2
    own_ref, peer_ref = refs[-2:]
    total = dot(refs[0][...], refs[count][...])
    for at in range(1, count):
        total = total + dot(refs[at][...], refs[count + at][...])
    half = own_ref.shape[0]
    own_ref[...] = total[:half]
    peer_ref[...] = total[half:].astype(bf16)


def cotangent_kernel(*refs):
    count = (len(refs) - 5) // 2
    mine_ref, other_ref, own_ref, peer_ref, gain_ref = refs[-5:]
    total = dot(refs[0][...], refs[count][...], (1, 1))
    for at in range(1, count):
        total = total + dot(refs[at][...], refs[count + at][...], (1, 1))
    half = own_ref.shape[0]
    own_ref[...] = total[:half]
    peer_ref[...] = total[half:].astype(bf16)
    gain = jnp.sum(
        total[:half] * mine_ref[...].astype(f32) + total[half:] * other_ref[...].astype(f32),
        axis=0,
        keepdims=True,
    )
    gain_ref[...] = jnp.broadcast_to(gain, gain_ref.shape)


def run_sum(kernel, left, right, turned, normed=()):
    rows, width = left[0].shape[0], right[0].shape[0] if turned else right[0].shape[1]
    tile = 512
    half = rows // 2
    columns = pl.BlockSpec((half, tile), lambda step: (0, step))
    specs = [whole(array) for array in left]
    for array in right:
        if turned:
            specs.append(pl.BlockSpec((tile, array.shape[1]), lambda step: (step, 0)))
        else:
            specs.append(pl.BlockSpec((array.shape[0], tile), lambda step: (0, step)))
    shapes = [jax.ShapeDtypeStruct((half, width), f32), jax.ShapeDtypeStruct((half, width), bf16)]
    outs = [columns, columns]
    if normed:
        specs = specs + [columns, columns]
        shapes.append(jax.ShapeDtypeStruct((sub, width), f32))
        outs.append(pl.BlockSpec((sub, tile), lambda step: (0, step)))
    return pl.pallas_call(
        kernel,
        grid=(width // tile,),
        in_specs=specs,
        out_specs=outs,
        out_shape=shapes,
        compiler_params=call_params(),
    )(*left, *right, *normed)


def sum_over(values, axis, count):
    if count & (count - 1):
        return lax.psum(values, axis)
    mask = 1
    while mask < count:
        values = values + swap_by(values, axis, count, mask)
        mask = mask * 2
    return values


def shards(
    block_input,
    seq_lengths,
    cotangent,
    norm_gain,
    proj_zx,
    proj_dt,
    proj_bc,
    chan_params,
    conv_bc,
    head_params,
    out_proj,
    gain_moments,
    zx_moments,
    dt_moments,
    bc_moments,
    chan_moments,
    convbc_moments,
    head_moments,
    out_moments,
):
    heads_axis = lax.axis_size(HEAD)
    dp_axis = lax.axis_size(DP)
    slot_count = seq_lengths.shape[0]
    rows_own, model_width = block_input.shape
    rows_dev = rows_own * heads_axis
    seq_len = rows_dev // slot_count
    rows_dp = proj_zx.shape[0]
    inner = chan_params.shape[1]
    inner_all = inner * heads_axis
    heads_loc = head_params.shape[1]
    headdim = inner // heads_loc
    kernel = chan_params.shape[0] - 2
    state = conv_bc.shape[1] // 2
    spot = lax.axis_index(HEAD)
    place = lax.axis_index(DP).astype(jnp.int32).reshape(1)
    paired = heads_axis == 4 and dp_axis == 8 and rows_own == seq_len

    zx_low = proj_zx.astype(bf16)
    piece_a = jnp.concatenate([zx_low[:, 0], proj_bc.astype(bf16)], axis=1)
    piece_b = jnp.concatenate([zx_low[:, 1], pad_to(proj_dt.astype(bf16), rows_dp, lanes)], axis=1)
    out_low = out_proj.astype(bf16)
    taps = pad_to(
        jnp.concatenate([chan_params, jnp.repeat(head_params[2:3], headdim, axis=1)], axis=0),
        sub,
        inner,
    )
    cbc = pad_to(conv_bc, sub, 2 * state)
    table = jnp.concatenate([taps, pad_to(head_params, sub, lanes)], axis=1)

    positions = iota((slot_count, seq_len), 1)
    live_mask = (positions < seq_lengths[:, None]).astype(f32).reshape(rows_dev, 1)
    live_own = lax.dynamic_slice_in_dim(live_mask, spot * rows_own, rows_own, 0)
    gain_float = lax.optimization_barrier(norm_gain.astype(bf16)).astype(f32)
    input_float = block_input.astype(f32)
    inv_own = lax.rsqrt(jnp.mean(input_float * input_float, axis=-1, keepdims=True) + norm_eps)
    own_hat = input_float * inv_own
    normed_own = (own_hat * gain_float[None, :]).astype(bf16)
    cot_float = cotangent.astype(f32)
    cot_own = (cot_float * live_own).astype(bf16)
    tables = (table, cbc)

    if paired:
        more_a = swap_by(zx_low[:, 0], HEAD, 4, WEIGHT_PLACE)
        more_b = swap_by(piece_b, HEAD, 4, WEIGHT_PLACE)
        near_a = gather_near(piece_a, 2)
        near_b = gather_near(piece_b, 4)
        normed_all = (normed_own, swap_by(normed_own, HEAD, 4, TOKEN_PLACE))
        out_more_low = swap_by(out_low, HEAD, 4, WEIGHT_PLACE)
        tables_more = (swap_by(table, HEAD, 4, WEIGHT_PLACE), cbc)
        own_pieces = (gather_rest(piece_a, *near_a, 2), gather_rest(piece_b, *near_b, 4))
        more_a, more_b = after((more_a, more_b), *own_pieces[0], *own_pieces[1])
        near_a = gather_near(more_a, 2)
        near_b = gather_near(more_b, 4)
        more_pieces = (gather_rest(more_a, *near_a, 2), gather_rest(more_b, *near_b, 4))
        out_low, out_more_low = after((out_low, out_more_low), *near_a, *near_b)
        near_a = gather_near(out_low, 2)
        near_b = gather_near(out_more_low, 4)
        out_pieces = (gather_rest(out_low, *near_a, 2), gather_rest(out_more_low, *near_b, 4))
        cot_all = (cot_own, swap_by(cot_own, HEAD, 4, TOKEN_PLACE))
        proj_a, proj_b, plain, gated, own_a, own_b, turned = run_forward(
            place, normed_all, own_pieces, None, tables, seq_len, state, kernel
        )
        more_proj_a, more_proj_b, more_plain, more_gated, more_a, more_b = run_forward(
            place, normed_all, more_pieces, proj_a, tables_more, seq_len, state, kernel
        )
        grad, more_grad, stats, lifted_turned, lifted, more_lifted, out_a, out_b = run_gate(
            place, cot_all, out_pieces, (gated, more_gated), (table, tables_more[0]), seq_len, kernel
        )
        stat_parts = [stats, swap_by(stats, HEAD, 4, TOKEN_PLACE)]
        out_own = run_product(
            place, lifted_turned, cot_all, order_of(2), stat_parts, 0, 2, inner_all
        )
        out_more = run_product(
            place, lifted_turned, cot_all, order_of(4), stat_parts, 1, 2, inner_all
        )
        lifted, more_lifted = after((lifted, more_lifted), out_own[0], out_more[0])
        branch_own, branch_peer = run_sum(
            branch_kernel, (lifted, more_lifted), (out_a, out_b), False
        )
        branch_own = branch_own + swap_by(branch_peer, HEAD, 4, TOKEN_PLACE).astype(f32)
        square_own = stats[:1] + stat_parts[1][sub : sub + 1]
        gate_own = lax.rsqrt(square_own / inner_all + norm_eps).reshape(seq_len, 1)
        out_own = scatter_first(*out_own)
        out_more = scatter_first(*out_more)
        more_grad = after(more_grad, branch_peer, out_own[0], out_more[0])
        more_cot_a, more_cot_b, more_sums, bc_part = run_backward(
            stat_parts,
            True,
            (more_proj_a, more_proj_b),
            proj_a,
            None,
            more_plain,
            more_grad,
            tables_more,
            seq_len,
            state,
            kernel,
            inner_all,
        )
        grad_more_a = run_product(place, turned, (more_cot_a,), order_of(2))
        grad_more_b = run_product(place, turned, (more_cot_b,), order_of(4))
        out_own = scatter_second(*out_own, 2)
        out_more = scatter_second(*out_more, 4)
        grad = after(grad, grad_more_a[0], grad_more_b[0], out_own[0], out_more[0])
        cot_a, cot_b, own_sums, cbc_sums = run_backward(
            stat_parts,
            True,
            (proj_a, proj_b),
            None,
            bc_part,
            plain,
            grad,
            tables,
            seq_len,
            state,
            kernel,
            inner_all,
        )
        grad_more_a = scatter_first(*grad_more_a)
        grad_more_b = scatter_first(*grad_more_b)
        out_away = scatter_third(*out_more, 4).astype(bf16)
        cot_a, cot_b = after((cot_a, cot_b), out_away, grad_more_a[0], grad_more_b[0])
        grad_own_a = run_product(place, turned, (cot_a,), order_of(2))
        grad_own_b = run_product(place, turned, (cot_b,), order_of(4))
        grad_more_a = scatter_second(*grad_more_a, 2)
        grad_more_b = scatter_second(*grad_more_b, 4)
        grad_own_a = scatter_first(*grad_own_a)
        grad_own_b = scatter_first(*grad_own_b)
        cot_a, cot_b, more_cot_a, more_cot_b = after(
            (cot_a, cot_b, more_cot_a, more_cot_b),
            grad_more_a[0],
            grad_more_b[0],
            grad_own_a[0],
            grad_own_b[0],
        )
        grad_out = scatter_third(*out_own, 2) + swap_by(out_away, HEAD, 4, WEIGHT_PLACE).astype(f32)
        cot_whole, cot_peer, grad_gain = run_sum(
            cotangent_kernel,
            (more_cot_a, more_cot_b, cot_a, cot_b),
            (more_a, more_b, own_a, own_b),
            True,
            normed_all,
        )
        cot_whole = cot_whole + swap_by(cot_peer, HEAD, 4, TOKEN_PLACE).astype(f32)
        away_a = scatter_third(*grad_more_a, 2).astype(bf16)
        away_b = scatter_third(*grad_more_b, 4).astype(bf16)
        home_a = swap_by(away_a, HEAD, 4, WEIGHT_PLACE)
        home_b = swap_by(away_b, HEAD, 4, WEIGHT_PLACE)
        grad_own_a = scatter_second(*grad_own_a, 2)
        grad_own_b = scatter_second(*grad_own_b, 4)
        terms_a = scatter_last(*grad_own_a, 2)
        terms_b = scatter_last(*grad_own_b, 4)
        zx_next, zx_state, dt_next, dt_state = run_adam(
            terms_a, terms_b, home_a, home_b, (proj_zx, zx_moments, proj_dt, dt_moments), inner
        )
        grad_bc = wide_sum(*[term[0, :, inner:] for term in terms_a[:-1]], terms_a[-1][:, inner:])
        bc_low = grad_bc.astype(bf16)
        for mask in (1, 2, 3):
            grad_bc = grad_bc + swap_by(bc_low, HEAD, 4, mask).astype(f32)
        wide = inner + lanes
        small = jnp.concatenate([more_sums, own_sums, cbc_sums, grad_gain], axis=1)
        small = small + swap_by(small, DP, 8, 1)
        small = small + sum(swap_by(small, DP, 8, mask) for mask in (2, 4, 6))
        both = small[:, 2 * wide :]
        both = both + sum(swap_by(both, HEAD, 4, mask) for mask in (1, 2, 3))
        own_sums = small[:, wide : 2 * wide] + swap_by(small[:, :wide], HEAD, 4, WEIGHT_PLACE)
        cbc_sums, grad_gain = both[:, : 2 * state], both[0, 2 * state :]
    else:
        normed_all = lax.all_gather(normed_own, HEAD, axis=0, tiled=True)
        cot_all = lax.all_gather(cot_own, HEAD, axis=0, tiled=True)
        own_a = lax.all_gather(piece_a, DP, axis=0, tiled=True)
        own_b = lax.all_gather(piece_b, DP, axis=0, tiled=True)
        out_full = lax.all_gather(out_low, DP, axis=0, tiled=True)
        proj_a, proj_b, plain, gated = run_forward(
            None, (normed_all,), (own_a, own_b), None, tables, seq_len, state, kernel
        )
        grad, stats, _, lifted = run_gate(
            None, (cot_all,), (out_full,), (gated,), (table,), seq_len, kernel
        )
        branch = dot(lifted, out_full)
        stats = lax.psum(stats, HEAD)
        square = stats.reshape(slot_count, sub, seq_len)[:, 0].reshape(rows_dev, 1)
        gate_all = lax.rsqrt(square / inner_all + norm_eps)
        gate_own = lax.dynamic_slice_in_dim(gate_all, spot * rows_own, rows_own, 0)
        cot_gate = (cot_all.astype(f32) * gate_all).astype(bf16)
        cot_a, cot_b, own_sums, cbc_sums = run_backward(
            [stats],
            False,
            (proj_a, proj_b),
            None,
            None,
            plain,
            grad,
            tables,
            seq_len,
            state,
            kernel,
            inner_all,
        )
        cot_input = dot(cot_a, own_a, (1, 1)) + dot(cot_b, own_b, (1, 1))
        grad_gain = jnp.sum(cot_input * normed_all.astype(f32), axis=0)

        def scatter(values, axis):
            return lax.psum_scatter(
                values.astype(bf16), axis, scatter_dimension=0, tiled=True
            ).astype(f32)

        cot_whole = scatter(cot_input, HEAD)
        branch_own = scatter(branch, HEAD)
        grad_out = scatter(dot(lifted, cot_gate, (0, 0)), DP)
        sum_a = scatter(dot(normed_all, cot_a, (0, 0)), DP)
        sum_b = scatter(dot(normed_all, cot_b, (0, 0)), DP)
        grad_zx = jnp.stack([sum_a[:, :inner], sum_b[:, :inner]], axis=1)
        grad_dt = sum_b[:, inner:][:, :heads_loc]
        zx_next, zx_state = adam_update(proj_zx, zx_moments, grad_zx, rate_matrix, weight_decay)
        dt_next, dt_state = adam_update(proj_dt, dt_moments, grad_dt, rate_matrix, weight_decay)
        grad_bc = lax.psum(sum_a[:, inner:].astype(bf16), HEAD).astype(f32)
        own_sums = sum_over(own_sums, DP, dp_axis)
        cbc_sums = sum_over(sum_over(cbc_sums, DP, dp_axis), HEAD, heads_axis)
        grad_gain = sum_over(sum_over(grad_gain, DP, dp_axis), HEAD, heads_axis)

    block_output = (input_float + live_own * (branch_own * gate_own)).astype(bf16)
    lift_own = cot_whole * gain_float[None, :]
    row_dot = jnp.sum(lift_own * own_hat, axis=-1, keepdims=True)
    input_grad = cot_float + inv_own * (lift_own - own_hat * row_dot / model_width)

    grad_convbc = cbc_sums[: kernel + 1]
    grad_gain = grad_gain / gain_float
    grad_chan = own_sums[: kernel + 2, :inner]
    grad_skip = jnp.sum(own_sums[kernel + 2, :inner].reshape(heads_loc, headdim), axis=1)
    grad_head = jnp.concatenate(
        [own_sums[:2, inner : inner + heads_loc], grad_skip[None, :]], axis=0
    )

    gain_next, gain_state = adam_update(norm_gain, gain_moments, grad_gain, rate_vector, 0.0)
    bc_next, bc_state = adam_update(proj_bc, bc_moments, grad_bc, rate_matrix, weight_decay)
    chan_next, chan_state = adam_update(chan_params, chan_moments, grad_chan, rate_vector, 0.0)
    convbc_next, convbc_state = adam_update(conv_bc, convbc_moments, grad_convbc, rate_vector, 0.0)
    head_next, head_state = adam_update(head_params, head_moments, grad_head, rate_vector, 0.0)
    outproj_next, outproj_state = adam_update(
        out_proj, out_moments, grad_out, rate_matrix, weight_decay
    )
    return (
        block_output,
        input_grad,
        gain_next,
        gain_state,
        zx_next,
        zx_state,
        dt_next,
        dt_state,
        bc_next,
        bc_state,
        chan_next,
        chan_state,
        convbc_next,
        convbc_state,
        head_next,
        head_state,
        outproj_next,
        outproj_state,
    )


def solution(mesh):
    placed = (
        P((DP, HEAD), None),
        P(DP),
        P((DP, HEAD), None),
        P(),
        P(DP, None, HEAD),
        P(DP, HEAD),
        P(DP, None),
        P(None, HEAD),
        P(),
        P(None, HEAD),
        P((HEAD, DP), None),
        P(),
        P(None, DP, None, HEAD),
        P(None, DP, HEAD),
        P(None, DP, None),
        P(None, None, HEAD),
        P(),
        P(None, None, HEAD),
        P(None, (HEAD, DP), None),
    )
    return jax.shard_map(
        shards,
        mesh=mesh,
        in_specs=placed,
        out_specs=(
            P((DP, HEAD), None),
            P((DP, HEAD), None),
            P(),
            P(),
            P(DP, None, HEAD),
            P(None, DP, None, HEAD),
            P(DP, HEAD),
            P(None, DP, HEAD),
            P(DP, None),
            P(None, DP, None),
            P(None, HEAD),
            P(None, None, HEAD),
            P(),
            P(),
            P(None, HEAD),
            P(None, None, HEAD),
            P((HEAD, DP), None),
            P(None, (HEAD, DP), None),
        ),
        check_vma=False,
    )
```
